1024 devices in a mesh: section: 8 (over x), ctx: 8 (over z), exp: 16 (over y, core).
Axes of the slice: x: 8, y: 8, z: 8, core: 2. Of those that a mesh axis runs over, the one named last changes fastest.
Arguments:
- queries: bfloat16 [8, 2048, 8192], P('section', 'ctx', 'exp'), may hold values from -0.8984375 to 0.8984375
- keys_in: bfloat16 [8, 2048, 8192], P('section', 'ctx', 'exp'), may hold values from -0.8984375 to 0.8984375
- values: bfloat16 [8, 2048, 8192], P('section', 'ctx', 'exp'), may hold values from -6 to 6
- decay_rate: float32 [8, 64, 2048], P('section', 'exp', 'ctx'), may hold values from 0 to 1
- out_weight: bfloat16 [8, 8192, 6144], P('section', 'exp'), may hold values from -0.0625 to 0.0625
- residual: bfloat16 [8, 2048, 6144], P('section', ('ctx', 'exp')), may hold values from -6 to 6
- norm_gain: float32 [8, 6144], P('section'), may hold values from 0.5 to 1.5
- router: bfloat16 [8, 6144, 16], P('section'), may hold values from -0.078125 to 0.078125
- expert_ids: int32 [8, 2048, 2], P('section', ('ctx', 'exp')), may hold values from 0 to 15, all different within a row; in each aligned block of 16 rows (0 to 15, 16 to 31, ..., all dimensions but the last counted through in order) at most 4 rows name the same one
Outputs:
- expert_rows: bfloat16 [8, 8, 16, 16, 4, 6144], P('section', 'ctx', 'exp')
- expert_gates: bfloat16 [8, 8, 16, 16, 4], P('section', 'ctx', 'exp')
The draws below stay inside these ranges and needn't reach their ends.
Inputs may be any that keep to these rules, and one draw needn't show every extreme that they name: `expert_ids`: in each device's 16 rows, every row names two different experts, no expert is named more than 4 times, and in some devices' rows an expert is named exactly 4 times.
All inputs are finite; a program needn't handle non-finite values.
Results may differ from the reference program's by a relative error of at most 0.02.
Values may be sent and summed in bfloat16 or wider, within the bound.
A program may use at most 64 MiB of HBM per device.

```python
import math
import jax
import jax.numpy as jnp
import numpy as np
from jax import lax

D = 6144
HEAD_DIM = 128
HEAD_DEV = 4
EXPERTS = 16
TOK_SHARE = 16
L_DEV = 256
SEQUENCE_LENGTH = 2048
HEADS = 64
CAP = 4
N_SECTION = 8
N_CTX = 8
N_EXP = 16


def draw_decay_rate(key, part):
    key_rows = jax.random.split(key, 6)
    slow_share = 0.5
    head_shape = (N_SECTION, HEADS, 1)
    complete_shape = (N_SECTION, HEADS, SEQUENCE_LENGTH)
    slow = jax.random.uniform(key_rows[0], head_shape) < slow_share
    fast_rate = jnp.exp(jax.random.uniform(key_rows[1], head_shape, minval=jnp.log(1.0 / 50.0), maxval=jnp.log(1.0 / 30.0)))
    slow_rate = jnp.exp(jax.random.uniform(key_rows[2], head_shape, minval=jnp.log(0.1 / SEQUENCE_LENGTH), maxval=jnp.log(0.8 / SEQUENCE_LENGTH)))
    baseline_decay = jnp.where(slow, slow_rate, fast_rate)
    coarse_estimate = jax.random.uniform(key_rows[3], complete_shape, minval=0.5, maxval=1.5)
    spike_position = jax.random.uniform(key_rows[4], complete_shape) < 2.0 / SEQUENCE_LENGTH
    spike_penalty = jax.random.uniform(key_rows[5], complete_shape, minval=0.2, maxval=0.45)
    return (baseline_decay * coarse_estimate + jnp.where(spike_position, -jnp.log(1.0 - spike_penalty), 0.0)).astype(jnp.float32)


def block_levels(stream_key, extent, cuts, low, high):
    gain = 1.0
    for position, shards_of in cuts:
        steps = jax.random.uniform(jax.random.fold_in(jax.random.fold_in(stream_key, 6), position), (shards_of,), jnp.float32, low / len(cuts), high / len(cuts))
        gain = gain * jnp.repeat(jnp.exp(steps), extent[position] // shards_of).reshape((-1,) + (1,) * (len(extent) - 1 - position))
    return gain


def shared_out(own_key, own, number, rows, count, top, bound, slope):
    sequence = jax.random.permutation(own_key, count)
    packed, ordinary = shares(count, rows * top, bound, slope, True), shares(count, rows * top, bound, slope, False)
    places = jnp.arange(count)

    def named(tallies, turn):
        used = int((tallies > 0).sum())
        fixed = max(1, used // 4)
        shifted = fixed + (places - fixed + turn * (used - fixed)) % max(1, count - fixed)
        return jnp.zeros((count,), jnp.int32).at[sequence[jnp.where(places < fixed, places, shifted)]].set(jnp.asarray(tallies, jnp.int32))

    tallies = jnp.where(number % 4 == 0, named(packed, number // 4), named(ordinary, number - number // 4 - 1))
    mixed = jax.random.permutation(jax.random.fold_in(own, 3), count)
    giver, taker = mixed[0:count // 2 * 2:2], mixed[1:count // 2 * 2:2]
    room = jnp.minimum(tallies[giver] - 1, bound - tallies[taker]) // 2
    room = jnp.where((giver == sequence[0]) | (taker == sequence[0]) | (tallies[taker] == 0), 0, jnp.maximum(room, 0))
    shifted = jax.random.randint(jax.random.fold_in(own, 4), (count // 2,), 0, 1 << 20) % (room + 1)
    tallies = tallies.at[giver].add(-shifted).at[taker].add(shifted)
    items = jnp.searchsorted(jnp.cumsum(tallies), jnp.arange(rows * top), side="right").astype(jnp.int32)
    listing = items.reshape(top, rows).T
    listing = listing[jax.random.permutation(jax.random.fold_in(own, 1), rows)]
    turn = jax.random.randint(jax.random.fold_in(own, 2), (rows, 1), 0, top)
    return jnp.take_along_axis(listing, (jnp.arange(top)[None, :] + turn) % top, axis=1)


def shares(count, total, reach, skew, full):
    loads = [(1 << 20) // math.isqrt(standing ** skew) + 1 for standing in range(1, count + 1)]
    largest = reach if full else min(reach, max(-(-total // count), total * loads[0] // sum(loads)))
    least = 1 if total - largest >= count - 1 else 0
    counts, surplus = [largest] + [least] * (count - 1), total - largest - least * (count - 1)
    while surplus > 0:
        free = [i for i in range(1, count) if counts[i] < largest] or [i for i in range(1, count) if counts[i] < reach]
        mass, left = sum([loads[i] for i in free]), surplus
        for i in free:
            extra = min(reach - counts[i], max(1, left * loads[i] // mass), surplus)
            counts[i] = counts[i] + extra
            surplus = surplus - extra
    return np.array(counts)


def scatter_about(stream_key, dims, deviation, most, cuts=(), kind=jnp.bfloat16):
    values = deviation * jax.random.normal(stream_key, dims, jnp.float32)
    if cuts:
        values = values * block_levels(stream_key, dims, cuts, -0.22, 0.18)
    return jnp.clip(values, -most, most).astype(kind)


def setup_inputs(seed: int = 0) -> dict:
    key_list = jax.random.split(jax.random.key(seed), 10)
    queries = scatter_about(key_list[0], (N_SECTION, SEQUENCE_LENGTH, HEADS * HEAD_DIM), 0.15, 0.8984375, ((0, 8), (1, 8), (2, 16)))
    keys_in = scatter_about(key_list[1], (N_SECTION, SEQUENCE_LENGTH, HEADS * HEAD_DIM), 0.15, 0.8984375, ((0, 8), (1, 8), (2, 16)))
    values = scatter_about(key_list[2], (N_SECTION, SEQUENCE_LENGTH, HEADS * HEAD_DIM), 1.0, 6.0, ((0, 8), (1, 8), (2, 16)))
    decay_rate = draw_decay_rate(jax.random.fold_in(key_list[9], 71), 0)
    out_weight = scatter_about(key_list[4], (N_SECTION, HEADS * HEAD_DIM, D), (HEADS * HEAD_DIM) ** -0.5, 0.0625, ((0, 8), (1, 16)))
    residual = scatter_about(key_list[5], (N_SECTION, SEQUENCE_LENGTH, D), 1.0, 6.0, ((0, 8), (1, 128)))
    norm_gain = jnp.clip(1.0 + 0.1 * jax.random.normal(key_list[6], (N_SECTION, D), jnp.float32), 0.5, 1.5)
    router = scatter_about(key_list[7], (N_SECTION, D, EXPERTS), D ** -0.5, 0.078125, ((0, 8),))
    expert_ids_keys = jax.random.split(jax.random.fold_in(key_list[8], 1), N_SECTION * SEQUENCE_LENGTH // TOK_SHARE)
    expert_ids_turns = jax.random.permutation(jax.random.fold_in(key_list[8], 3), N_SECTION * SEQUENCE_LENGTH // TOK_SHARE)
    expert_ids = jax.vmap(lambda own, number: shared_out(jax.random.fold_in(key_list[8], 2), own, number, TOK_SHARE, EXPERTS, 2, CAP, 2))(expert_ids_keys, expert_ids_turns).reshape((N_SECTION, SEQUENCE_LENGTH, 2))
    return {"queries": queries, "keys_in": keys_in, "values": values, "decay_rate": decay_rate, "out_weight": out_weight, "residual": residual, "norm_gain": norm_gain, "router": router, "expert_ids": expert_ids}


precise = lax.Precision.HIGHEST
epsilon = 1e-05

def block_attention(queries, keys_in, values, decay_rate):
    shaped_q = queries.reshape(N_CTX, L_DEV, HEADS, HEAD_DIM).astype(jnp.float32)
    shaped_k = keys_in.reshape(N_CTX, L_DEV, HEADS, HEAD_DIM).astype(jnp.float32)
    shaped_v = values.reshape(N_CTX, L_DEV, HEADS, HEAD_DIM).astype(jnp.float32)
    cum_log = jnp.cumsum(-decay_rate.reshape(HEADS, N_CTX, L_DEV), axis=-1)
    attention_logits = jnp.einsum('nlhd,nmhd->hnlm', shaped_q, shaped_k)
    log_gap = cum_log[:, :, :, None] - cum_log[:, :, None, :]
    causal = jnp.arange(L_DEV, dtype=jnp.int32)[:, None] >= jnp.arange(L_DEV, dtype=jnp.int32)[None, :]
    weight_matrix = jnp.where(causal, attention_logits * jnp.exp(jnp.minimum(log_gap, 0.0)), 0.0).astype(jnp.bfloat16)
    inner_part = jnp.einsum('hnlm,nmhd->nlhd', weight_matrix.astype(jnp.float32), shaped_v)
    tail_decay = jnp.exp(cum_log[:, :, -1:] - cum_log)
    keyed_rows = shaped_k * jnp.transpose(tail_decay, (1, 2, 0))[:, :, :, None]
    local_state = jnp.einsum('nlha,nlhb->nhab', keyed_rows, shaped_v, precision=precise)
    total_log = jnp.transpose(cum_log[:, :, -1])

    def advance(carried, piece):
        block_log, block_state = piece
        return (jnp.exp(block_log)[:, None, None] * carried + block_state, carried)
    start_state = jnp.zeros((HEADS, HEAD_DIM, HEAD_DIM), jnp.float32)
    unused, incoming = lax.scan(advance, start_state, (total_log, local_state))
    outside = jnp.exp(jnp.transpose(cum_log, (1, 2, 0)))[:, :, :, None] * jnp.einsum('nlhd,nhde->nlhe', shaped_q, incoming, precision=precise)
    return (inner_part + outside).astype(jnp.bfloat16).reshape(SEQUENCE_LENGTH, HEADS * HEAD_DIM)

def project_heads(attended, out_weight):
    grouped = attended.reshape(SEQUENCE_LENGTH, N_EXP, HEAD_DEV * HEAD_DIM)
    grouped_w = out_weight.reshape(N_EXP, HEAD_DEV * HEAD_DIM, D)

    def add_group(running, index):
        term = jnp.dot(grouped[:, index], grouped_w[index], preferred_element_type=jnp.float32)
        rounded = lax.optimization_barrier(term.astype(jnp.bfloat16))
        return (running + rounded.astype(jnp.float32), None)
    summed, unused = lax.scan(add_group, jnp.zeros((SEQUENCE_LENGTH, D), jnp.float32), jnp.arange(N_EXP, dtype=jnp.int32))
    return summed

def section_layer(piece):
    queries, keys_in, values, decay_rate, out_weight, residual = piece
    attended = block_attention(queries, keys_in, values, decay_rate)
    summed = project_heads(attended, out_weight)
    return (residual.astype(jnp.float32) + summed).astype(jnp.bfloat16)

def dispatch_section(piece):
    normed_s, ids_s, gates_s = piece
    blocks = N_CTX * N_EXP
    doubled = jnp.repeat(normed_s.reshape(blocks, TOK_SHARE, D), 2, axis=1)
    flat_ids = ids_s.reshape(blocks, 2 * TOK_SHARE)
    onehot = (flat_ids[:, :, None] == jnp.arange(EXPERTS, dtype=jnp.int32)[None, None, :]).astype(jnp.int32)
    slot_rank = lax.optimization_barrier(jnp.sum((jnp.cumsum(onehot, axis=1) - onehot) * onehot, axis=-1)).astype(jnp.int32)
    target = (flat_ids * CAP + slot_rank).astype(jnp.int32)
    placement = (target[:, None, :] == jnp.arange(EXPERTS * CAP, dtype=jnp.int32)[None, :, None]).astype(jnp.float32)
    rows = jnp.einsum('bsa,bad->bsd', placement, doubled.astype(jnp.float32)).astype(jnp.bfloat16)
    gate_rows = jnp.einsum('bsa,ba->bs', placement, gates_s.reshape(blocks, 2 * TOK_SHARE).astype(jnp.float32)).astype(jnp.bfloat16)
    rows = jnp.transpose(rows.reshape(N_CTX, N_EXP, EXPERTS, CAP, D), (0, 2, 1, 3, 4))
    gate_rows = jnp.transpose(gate_rows.reshape(N_CTX, N_EXP, EXPERTS, CAP), (0, 2, 1, 3))
    return (rows, gate_rows)

def reference(queries, keys_in, values, decay_rate, out_weight, residual, norm_gain, router, expert_ids):
    hidden = lax.map(section_layer, (queries, keys_in, values, decay_rate, out_weight, residual))
    received = jnp.roll(hidden, 1, axis=0)
    wide = received.astype(jnp.float32)
    mean_sq = lax.optimization_barrier(jnp.mean(wide * wide, axis=-1, keepdims=True))
    normed = (wide * lax.rsqrt(mean_sq + epsilon) * norm_gain[:, None, :]).astype(jnp.bfloat16)
    logits = jnp.einsum('std,sde->ste', normed.astype(jnp.float32), router.astype(jnp.float32))
    expert_table = jnp.arange(EXPERTS, dtype=jnp.int32)
    picked = lax.optimization_barrier(jnp.sum(jnp.where(expert_ids[:, :, :, None] == expert_table, logits[:, :, None, :], 0.0), axis=-1))
    first_gate = jax.nn.sigmoid(picked[:, :, 0] - picked[:, :, 1])
    gate_pair = jnp.stack([first_gate, 1.0 - first_gate], axis=-1).astype(jnp.bfloat16)
    expert_rows, expert_gates = lax.map(dispatch_section, (normed, expert_ids, gate_pair))
    return (expert_rows, expert_gates)
```

```python
import functools

import jax
import jax.numpy as jnp
from jax import lax
from jax.experimental import pallas as pl
from jax.experimental.pallas import tpu as pltpu
from jax.sharding import PartitionSpec as P

HEAD_DIM = 128
HEAD_DEV = 4
CAP = 4
EPS = 1e-05
COLS = 256
MESH = pl.DeviceIdType.MESH
F32 = jnp.float32
BF16 = jnp.bfloat16


def iota(shape, dim):
    return lax.broadcasted_iota(jnp.int32, shape, dim)


def remote(src, dst, send_sem, recv_sem, **device):
    return pltpu.make_async_remote_copy(
        src_ref=src,
        dst_ref=dst,
        send_sem=send_sem,
        recv_sem=recv_sem,
        device_id=device,
        device_id_type=MESH,
    )


def contract(a, b, dims, **kw):
    return lax.dot_general(a, b, (dims, ((), ())), preferred_element_type=F32, **kw)


def kernel(
    sizes,
    q_hbm,
    k_hbm,
    v_hbm,
    decay_hbm,
    w_hbm,
    res_hbm,
    gain_hbm,
    router_hbm,
    ids_hbm,
    raw,
    meta,
    q_ref,
    k_ref,
    v_ref,
    decay_ref,
    res_ref,
    gain_ref,
    router_ref,
    ids_ref,
    weights,
    inner,
    attended,
    att_in,
    prod,
    state_out,
    state_in,
    scan_out,
    scan_in,
    ring_out,
    ring_in,
    shift_out,
    shift_in,
    placed,
    picks,
    squares,
    meta_out,
    load_sem,
    pair_send,
    pair_recv,
    z_send,
    z_recv,
    ring_send,
    ring_recv,
    shift_send,
    shift_recv,
    slot_send,
    slot_recv,
    meta_send,
    meta_recv,
    own_sem,
):
    n_sec, n_ctx, n_exp, length, width, cols = sizes
    n_y = n_exp // 2
    half = n_y // 2
    quarter = width // 4
    chunks = quarter // cols
    sec = lax.axis_index("section")
    ctx = lax.axis_index("ctx")
    exp = lax.axis_index("exp")
    y = exp // 2
    core = exp % 2

    def exp_at(dy, flip=0):
        there = (y + dy + n_y) % n_y
        side = 1 - core if flip else core
        return there * 2 + side

    loads = [
        pltpu.make_async_copy(src, dst, load_sem.at[i])
        for i, (src, dst) in enumerate(
            (
                (decay_hbm, decay_ref),
                (k_hbm, k_ref),
                (v_hbm, v_ref),
                (q_hbm, q_ref),
                (ids_hbm, ids_ref),
                (w_hbm, weights.at[0]),
                (res_hbm, res_ref),
                (gain_hbm, gain_ref),
                (router_hbm, router_ref),
            )
        )
    ]
    for load in loads:
        load.start()

    barrier = pltpu.get_barrier_semaphore()
    partners = 0
    for d in range(1, n_exp):
        pl.semaphore_signal(
            barrier, inc=1, device_id={"exp": (exp + d) % n_exp}, device_id_type=MESH
        )
        partners += 1
    for d in range(1, n_ctx):
        pl.semaphore_signal(
            barrier, inc=1, device_id={"ctx": (ctx + d) % n_ctx}, device_id_type=MESH
        )
        partners += 1
    if n_sec > 1:
        for d in (1, n_sec - 1):
            pl.semaphore_signal(
                barrier, inc=1, device_id={"section": (sec + d) % n_sec}, device_id_type=MESH
            )
            partners += 1

    loads[0].wait()
    lower = (iota((length, length), 0) >= iota((length, length), 1)).astype(F32)
    decay = decay_ref[...]
    b_col = -contract(lower, decay, ((1,), (1,)), precision=lax.Precision.HIGHEST)
    b_row = -contract(decay, lower, ((1,), (1,)), precision=lax.Precision.HIGHEST)
    b_last = b_col[length - 1 :, :]
    tail = jnp.exp(b_last - b_col)
    loads[1].wait()
    loads[2].wait()
    rows = HEAD_DEV * HEAD_DIM // n_ctx
    per_head = max(HEAD_DIM // rows, 1)
    for h in range(HEAD_DEV):
        at = slice(h * HEAD_DIM, (h + 1) * HEAD_DIM)
        keyed = (k_ref[:, at].astype(F32) * tail[:, h : h + 1]).astype(BF16)
        state = contract(keyed, v_ref[:, at], ((0,), (0,)))
        if n_ctx > 1:
            total = jnp.broadcast_to(b_last[:, h : h + 1], (16, HEAD_DIM))
            high = total.astype(BF16).astype(F32)
            middle = (total - high).astype(BF16).astype(F32)
            low = total - high - middle
            line = iota((16, HEAD_DIM), 0)
            log_rows = jnp.where(line == 0, high, jnp.where(line == 1, middle, low)).astype(BF16)
            for p in range(per_head):
                j = h * per_head + p
                state_out[j, 0:rows, :] = state[p * rows : (p + 1) * rows].astype(BF16)
                state_out[j, rows : rows + 16, :] = log_rows

    pl.semaphore_wait(barrier, partners)

    far_first = sorted(range(1, n_ctx), key=lambda d: -min(d, n_ctx - d))

    def z_copy(phase, d, out, into, theirs):
        peer = (ctx + d) % n_ctx
        return remote(
            out.at[peer], into.at[theirs], z_send.at[phase, d], z_recv.at[phase, d], ctx=peer
        )

    if n_ctx > 1:
        for d in far_first:
            z_copy(0, d, state_out, state_in, ctx).start()
    pair_w = remote(
        w_hbm, weights.at[1], pair_send.at[0], pair_recv.at[0], exp=exp_at(0, 1)
    )
    pair_w.start()
    if n_ctx > 1:
        state_in[ctx] = state_out[ctx]

    loads[3].wait()
    causal = iota((length, length), 0) >= iota((length, length), 1)
    for h in range(HEAD_DEV):
        at = slice(h * HEAD_DIM, (h + 1) * HEAD_DIM)
        scores = contract(q_ref[:, at], k_ref[:, at], ((1,), (1,)))
        gap = b_col[:, h : h + 1] - b_row[h : h + 1, :]
        mix = jnp.where(causal, scores * jnp.exp(jnp.minimum(gap, 0.0)), 0.0).astype(BF16)
        inner[:, at] = jnp.dot(mix, v_ref[:, at], preferred_element_type=F32)

    tok = ids_ref.shape[0]
    loads[4].wait()
    ids = ids_ref[...]
    first_id, second_id = ids[:, 0:1], ids[:, 1:2]
    experts = iota((tok, n_exp), 1)
    is_first = (first_id == experts).astype(F32)
    is_second = (second_id == experts).astype(F32)
    match = is_first + is_second
    earlier = (iota((tok, tok), 0) > iota((tok, tok), 1)).astype(F32)
    rank = jnp.dot(earlier.astype(BF16), match.astype(BF16), preferred_element_type=F32)
    code = jnp.where(match > 0.5, rank, -1.0)
    code4 = jnp.concatenate([code] * 4, axis=0)
    slot_rows = n_exp * 16
    spread = (iota((slot_rows, n_exp), 0) // 16 == iota((slot_rows, n_exp), 1)).astype(BF16)
    codes = contract(spread, code4.astype(BF16), ((1,), (1,)))
    line = iota((slot_rows, 4 * tok), 0) % 16
    part = iota((slot_rows, 4 * tok), 1) // tok
    picks[...] = jnp.where(
        jnp.logical_and(codes == (line % CAP).astype(F32), part == line // CAP), 1.0, 0.0
    ).astype(BF16)

    if n_ctx > 1:
        for d in far_first:
            z_copy(0, d, state_out, state_in, (ctx - d + n_ctx) % n_ctx).wait_recv()
        carried = jnp.zeros((rows, HEAD_DIM), F32)
        for n in range(n_ctx):
            scan_out[n] = carried.astype(BF16)
            if n < n_ctx - 1:
                logs = state_in[n, rows : rows + 16, :].astype(F32)
                total = logs[0:1] + logs[1:2] + logs[2:3]
                carried = jnp.exp(total) * carried + state_in[n, 0:rows, :].astype(F32)
        for d in far_first:
            z_copy(1, d, scan_out, scan_in, ctx).start()
        scan_in[ctx] = scan_out[ctx]
        for d in far_first:
            z_copy(1, d, scan_out, scan_in, (ctx - d + n_ctx) % n_ctx).wait_recv()

    grow = jnp.exp(b_col)
    for h in range(HEAD_DEV):
        at = slice(h * HEAD_DIM, (h + 1) * HEAD_DIM)
        whole = inner[:, at]
        if n_ctx > 1:
            pieces = [scan_in[h * per_head + p] for p in range(per_head)]
            incoming = jnp.concatenate(pieces, axis=0) if per_head > 1 else pieces[0]
            carried = jnp.dot(q_ref[:, at], incoming, preferred_element_type=F32)
            whole = whole + grow[:, h : h + 1] * carried
        split = whole.astype(BF16).reshape(n_y, 2, tok, HEAD_DIM)
        for c in range(2):
            attended[c, :, at] = split[:, c].reshape(n_y * tok, HEAD_DIM)
    pair_a = remote(
        attended.at[1 - core], att_in, pair_send.at[1], pair_recv.at[1], exp=exp_at(0, 1)
    )
    pair_a.start()
    loads[5].wait()
    loads[6].wait()
    pair_w.wait_recv()
    pair_a.wait_recv()

    right, left = exp_at(1), exp_at(-1)
    span = 2 * tok

    def ring_copy(way, step, i):
        src, dst = ring_out.at[way, step, i], ring_in.at[way, step, i]
        if step == 0:
            src, dst = src.at[pl.ds(way * span, span)], dst.at[pl.ds(way * span, span)]
        return remote(
            src,
            dst,
            ring_send.at[way, step, i],
            ring_recv.at[way, step, i],
            exp=left if way else right,
        )

    def dest(way, step):
        away = half - step
        return (y - away + n_y) % n_y if way else (y + away) % n_y

    @pl.loop(0, chunks)
    def _(i):
        mine, theirs = attended[core], att_in[...]
        for c in range(4):
            at = pl.ds(pl.multiple_of(c * quarter + i * cols, 128), cols)
            term = jnp.dot(mine, weights[0, :, at], preferred_element_type=F32)
            term = term + jnp.dot(theirs, weights[1, :, at], preferred_element_type=F32)
            prod[i, :, c * tok : (c + 1) * tok, :] = term.reshape(n_y, tok, cols)
        for way in range(2):
            part = slice(way * span, (way + 1) * span)
            ring_out[way, 0, i, part, :] = prod[i, dest(way, 0), part, :].astype(BF16)
            ring_copy(way, 0, i).start()

    for step in range(1, half):

        @pl.loop(0, chunks)
        def _(i, step=step):
            for way in range(2):
                ring_copy(way, step - 1, i).wait_recv()
                to = dest(way, step)
                if step == 1:
                    for p in range(2):
                        part = slice(p * span, (p + 1) * span)
                        total = prod[i, to, part, :]
                        if p == way:
                            total = total + ring_in[way, 0, i, part, :].astype(F32)
                        ring_out[way, 1, i, part, :] = total.astype(BF16)
                else:
                    total = prod[i, to] + ring_in[way, step - 1, i].astype(F32)
                    ring_out[way, step, i] = total.astype(BF16)
                ring_copy(way, step, i).start()

    def shift_copy(i):
        return remote(
            shift_out.at[i],
            shift_in.at[i],
            shift_send.at[i],
            shift_recv.at[i],
            section=(sec + 1) % n_sec,
        )

    def slot_copy(i, dy, flip, sender):
        peer = exp_at(dy, flip)
        k = dy * 2 + flip
        return remote(
            placed.at[i, peer], raw.at[sender, i], slot_send.at[i, k], slot_recv.at[i, k], exp=peer
        )

    def own_copy(i):
        return pltpu.make_async_copy(placed.at[i, exp], raw.at[exp, i], own_sem.at[i])

    order = sorted(range(1, n_y), key=lambda d: -min(d, n_y - d)) + [0]
    others = [(dy, flip) for dy in order for flip in (0, 1) if (dy, flip) != (0, 0)]

    squares[...] = jnp.zeros_like(squares)

    @pl.loop(0, chunks + 2)
    def _(i):
        @pl.when(i < chunks)
        def _():
            ring_copy(0, half - 1, i).wait_recv()
            ring_copy(1, half - 1, i).wait_recv()
            for c in range(4):
                part = slice(c * tok, (c + 1) * tok)
                at = pl.ds(pl.multiple_of(c * quarter + i * cols, 128), cols)
                total = prod[i, y, part, :]
                for way in range(2):
                    if half > 1 or way == c // 2:
                        total = total + ring_in[way, half - 1, i, part, :].astype(F32)
                total = total + res_ref[:, at].astype(F32)
                shift_out[i, part, :] = total.astype(BF16)
            if n_sec > 1:
                shift_copy(i).start()
            else:
                shift_in[i] = shift_out[i]

        @pl.when(i >= 2)
        def _():
            now = i - 2
            if n_sec > 1:
                shift_copy(now).wait_recv()
            rows_in = shift_in[now]
            wide = rows_in.astype(F32)
            squares[...] += jnp.sum(wide * wide, axis=-1, keepdims=True)
            slots = jnp.dot(picks[...], rows_in, preferred_element_type=F32)
            placed[now] = slots.astype(BF16).reshape(n_exp, 16, cols)
            for dy, flip in others:
                slot_copy(now, dy, flip, exp).start()
            own_copy(now).start()

    loads[7].wait()
    loads[8].wait()
    total = squares[0:tok, 0:1]
    for c in range(1, 4):
        total = total + squares[c * tok : (c + 1) * tok, 0:1]
    factor = lax.rsqrt(total / width + EPS)
    logits = jnp.zeros((tok, n_exp), F32)
    for c in range(4):
        for i in range(chunks):
            at = slice(c * quarter + i * cols, c * quarter + (i + 1) * cols)
            wide = shift_in[i, c * tok : (c + 1) * tok, :].astype(F32)
            normed = (wide * factor * gain_ref[:, at]).astype(BF16)
            logits = logits + jnp.dot(normed, router_ref[at, :], preferred_element_type=F32)
    picked0 = jnp.sum(logits * is_first, axis=-1, keepdims=True)
    picked1 = jnp.sum(logits * is_second, axis=-1, keepdims=True)
    gate0 = 1.0 / (1.0 + jnp.exp(picked1 - picked0))
    gate1 = 1.0 - gate0
    info_rows = n_exp * 2 * CAP
    spread8 = (iota((info_rows, n_exp), 0) // 8 == iota((info_rows, n_exp), 1)).astype(BF16)
    codes8 = contract(spread8, code.astype(BF16), ((1,), (1,)))
    first8 = contract(spread8, is_first.astype(BF16), ((1,), (1,)))
    diagonal = (iota((tok, tok), 0) == iota((tok, tok), 1)).astype(F32)

    def lying(column):
        return jnp.sum(diagonal * column, axis=0, keepdims=True)

    line8 = iota((info_rows, tok), 0) % 8
    gates = jnp.where(first8 > 0.5, lying(gate0), lying(gate1))
    info = jnp.where(line8 < CAP, lying(factor), gates)
    info = jnp.where(codes8 == (line8 % CAP).astype(F32), info, 0.0)
    info = jnp.sum(info, axis=-1, keepdims=True)
    meta_out[...] = jnp.broadcast_to(info, (info_rows, 128)).reshape(n_exp, 8, 128)

    def meta_copy(dy, flip, sender):
        peer = exp_at(dy, flip)
        k = dy * 2 + flip
        return remote(
            meta_out.at[peer], meta.at[sender], meta_send.at[k], meta_recv.at[k], exp=peer
        )

    own_meta = pltpu.make_async_copy(meta_out.at[exp], meta.at[exp], own_sem.at[chunks])
    for dy, flip in others:
        meta_copy(dy, flip, exp).start()
    own_meta.start()

    pair_w.wait_send()
    pair_a.wait_send()
    for d in far_first:
        for phase, (out, into) in enumerate(((state_out, state_in), (scan_out, scan_in))):
            z_copy(phase, d, out, into, ctx).wait_send()

    @pl.loop(0, chunks)
    def _(i):
        for way in range(2):
            for step in range(half):
                ring_copy(way, step, i).wait_send()
        if n_sec > 1:
            shift_copy(i).wait_send()
        own_copy(i).wait()
        for dy, flip in others:
            sender = exp_at(-dy, flip)
            slot_copy(i, dy, flip, exp).wait_send()
            slot_copy(i, dy, flip, sender).wait_recv()

    own_meta.wait()
    for dy, flip in others:
        meta_copy(dy, flip, exp).wait_send()
        meta_copy(dy, flip, exp_at(-dy, flip)).wait_recv()


def on_device(
    sizes, queries, keys_in, values, decay_rate, out_weight, residual, norm_gain, router, expert_ids
):
    n_sec, n_ctx, n_exp = sizes
    length, inner_width = queries.shape[1:]
    width = out_weight.shape[-1]
    tok = residual.shape[1]
    n_y = n_exp // 2
    half = n_y // 2
    quarter = width // 4
    cols = min(COLS, quarter // 2)
    chunks = quarter // cols
    rows = HEAD_DEV * HEAD_DIM // n_ctx
    any_space = pl.BlockSpec(memory_space=pl.ANY)
    dma = pltpu.SemaphoreType.DMA
    raw, meta = pl.pallas_call(
        functools.partial(kernel, (n_sec, n_ctx, n_exp, length, width, cols)),
        out_shape=(
            jax.ShapeDtypeStruct((n_exp, chunks, 16, cols), BF16),
            jax.ShapeDtypeStruct((n_exp, 8, 128), F32),
        ),
        in_specs=[any_space] * 9,
        out_specs=(any_space, any_space),
        scratch_shapes=[
            pltpu.VMEM((length, inner_width), BF16),
            pltpu.VMEM((length, inner_width), BF16),
            pltpu.VMEM((length, inner_width), BF16),
            pltpu.VMEM((HEAD_DEV, length), F32),
            pltpu.VMEM((tok, width), BF16),
            pltpu.VMEM((1, width), F32),
            pltpu.VMEM((width, n_exp), BF16),
            pltpu.VMEM((tok, 2), jnp.int32),
            pltpu.VMEM((2, inner_width, width), BF16),
            pltpu.VMEM((length, inner_width), F32),
            pltpu.VMEM((2, n_y * tok, inner_width), BF16),
            pltpu.VMEM((n_y * tok, inner_width), BF16),
            pltpu.VMEM((chunks, n_y, 4 * tok, cols), F32),
            pltpu.VMEM((n_ctx, rows + 16, HEAD_DIM), BF16),
            pltpu.VMEM((n_ctx, rows + 16, HEAD_DIM), BF16),
            pltpu.VMEM((n_ctx, rows, HEAD_DIM), BF16),
            pltpu.VMEM((n_ctx, rows, HEAD_DIM), BF16),
            pltpu.VMEM((2, half, chunks, 4 * tok, cols), BF16),
            pltpu.VMEM((2, half, chunks, 4 * tok, cols), BF16),
            pltpu.VMEM((chunks, 4 * tok, cols), BF16),
            pltpu.VMEM((chunks, 4 * tok, cols), BF16),
            pltpu.VMEM((chunks, n_exp, 16, cols), BF16),
            pltpu.VMEM((n_exp * 16, 4 * tok), BF16),
            pltpu.VMEM((4 * tok, 128), F32),
            pltpu.VMEM((n_exp, 8, 128), F32),
            dma((9,)),
            dma((2,)),
            dma((2,)),
            dma((2, n_ctx)),
            dma((2, n_ctx)),
            dma((2, half, chunks)),
            dma((2, half, chunks)),
            dma((chunks,)),
            dma((chunks,)),
            dma((chunks, n_exp)),
            dma((chunks, n_exp)),
            dma((n_exp,)),
            dma((n_exp,)),
            dma((chunks + 1,)),
        ],
        compiler_params=pltpu.CompilerParams(
            collective_id=0, has_side_effects=True, vmem_limit_bytes=56 * 2**20
        ),
    )(
        queries[0],
        keys_in[0],
        values[0],
        decay_rate[0],
        out_weight[0],
        residual[0],
        norm_gain,
        router[0],
        expert_ids[0],
    )
    factor = meta[:, 0:CAP, 0]
    gates = meta[:, CAP : 2 * CAP, 0].astype(BF16)
    rows_in = raw.reshape(n_exp, chunks, 4, CAP, cols).astype(F32)
    gain = norm_gain[0].reshape(4, chunks, cols).transpose(1, 0, 2)
    normed = (
        rows_in * factor[:, None, None, :, None] * gain[None, :, :, None, :]
    ).astype(BF16)
    normed = normed.transpose(0, 3, 2, 1, 4).reshape(n_exp, CAP, width)
    return (normed[None, None, None], gates[None, None, None])


def solution(mesh):
    sizes = tuple(mesh.shape[a] for a in ("section", "ctx", "exp"))
    placed = (
        P("section", "ctx", "exp"),
        P("section", "ctx", "exp"),
        P("section", "ctx", "exp"),
        P("section", "exp", "ctx"),
        P("section", "exp", None),
        P("section", ("ctx", "exp"), None),
        P("section", None),
        P("section", None, None),
        P("section", ("ctx", "exp"), None),
    )
    return jax.shard_map(
        functools.partial(on_device, sizes),
        mesh=mesh,
        in_specs=placed,
        out_specs=(
            P("section", "ctx", "exp", None, None, None),
            P("section", "ctx", "exp", None, None),
        ),
        check_vma=False,
    )
```

```python
import functools

import jax
import jax.numpy as jnp
from jax import lax
from jax.experimental import pallas as pl
from jax.experimental.pallas import tpu as pltpu
from jax.sharding import PartitionSpec as P

HEAD_DIM = 128
HEAD_DEV = 4
CAP = 4
EPS = 1e-05
COLS = 1024
RAW = 2
VMEM_MIB = 36
MESH = pl.DeviceIdType.MESH
F32 = jnp.float32
BF16 = jnp.bfloat16


def iota(shape, dim):
    return lax.broadcasted_iota(jnp.int32, shape, dim)


def remote(src, dst, send_sem, recv_sem, **device):
    return pltpu.make_async_remote_copy(
        src_ref=src,
        dst_ref=dst,
        send_sem=send_sem,
        recv_sem=recv_sem,
        device_id=device,
        device_id_type=MESH,
    )


def contract(a, b, dims, **kw):
    return lax.dot_general(a, b, (dims, ((), ())), preferred_element_type=F32, **kw)


def kernel(
    sizes,
    q_hbm,
    k_hbm,
    v_hbm,
    decay_hbm,
    w_hbm,
    res_hbm,
    gain_hbm,
    router_hbm,
    ids_hbm,
    rows_out,
    meta_in,
    q_ref,
    k_ref,
    v_ref,
    decay_ref,
    res_ref,
    gain_ref,
    router_ref,
    ids_ref,
    weights,
    inner,
    attended,
    att_in,
    prod,
    state_out,
    state_in,
    scan_out,
    scan_in,
    ring_out,
    ring_in,
    shift_out,
    shift_in,
    placed,
    picks,
    squares,
    meta_out,
    load_sem,
    pair_send,
    pair_recv,
    z_send,
    z_recv,
    ring_send,
    ring_recv,
    half_send,
    half_recv,
    shift_send,
    shift_recv,
    slot_send,
    slot_recv,
    meta_send,
    meta_recv,
    own_sem,
):
    n_sec, n_ctx, n_exp, length, width, cols = sizes
    n_y = n_exp // 2
    half = n_y // 2
    chunks = width // cols
    tok = length // n_exp
    sec = lax.axis_index("section")
    ctx = lax.axis_index("ctx")
    exp = lax.axis_index("exp")
    y = exp // 2
    core = exp % 2

    def exp_at(dy, flip=0):
        there = (y + dy + n_y) % n_y
        side = 1 - core if flip else core
        return there * 2 + side

    loads = [
        pltpu.make_async_copy(src, dst, load_sem.at[i])
        for i, (src, dst) in enumerate(
            (
                (decay_hbm, decay_ref),
                (k_hbm, k_ref),
                (v_hbm, v_ref),
                (q_hbm, q_ref),
                (ids_hbm, ids_ref),
                (w_hbm, weights.at[0]),
                (res_hbm, res_ref),
                (gain_hbm, gain_ref),
                (router_hbm, router_ref),
            )
        )
    ]
    for load in loads:
        load.start()

    barrier = pltpu.get_barrier_semaphore()
    partners = 0
    for d in range(1, n_exp):
        pl.semaphore_signal(
            barrier, inc=1, device_id={"exp": (exp + d) % n_exp}, device_id_type=MESH
        )
        partners += 1
    for d in range(1, n_ctx):
        pl.semaphore_signal(
            barrier, inc=1, device_id={"ctx": (ctx + d) % n_ctx}, device_id_type=MESH
        )
        partners += 1
    if n_sec > 1:
        for d in (1, n_sec - 1):
            pl.semaphore_signal(
                barrier, inc=1, device_id={"section": (sec + d) % n_sec}, device_id_type=MESH
            )
            partners += 1

    loads[0].wait()
    lower = (iota((length, length), 0) >= iota((length, length), 1)).astype(BF16)
    rest = -decay_ref[...]
    b_col = jnp.zeros((length, HEAD_DEV), F32)
    b_row = jnp.zeros((HEAD_DEV, length), F32)
    for _ in range(3):
        part = rest.astype(BF16)
        rest = rest - part.astype(F32)
        b_col = b_col + contract(lower, part, ((1,), (1,)))
        b_row = b_row + contract(part, lower, ((1,), (1,)))
    b_last = b_col[length - 1 :, :]
    tail = jnp.exp(b_last - b_col)
    loads[1].wait()
    loads[2].wait()
    rows = HEAD_DEV * HEAD_DIM // n_ctx
    per_head = max(HEAD_DIM // rows, 1)
    for h in range(HEAD_DEV):
        at = slice(h * HEAD_DIM, (h + 1) * HEAD_DIM)
        keyed = (k_ref[:, at].astype(F32) * tail[:, h : h + 1]).astype(BF16)
        state = contract(keyed, v_ref[:, at], ((0,), (0,)))
        if n_ctx > 1:
            total = jnp.broadcast_to(b_last[:, h : h + 1], (16, HEAD_DIM))
            high = total.astype(BF16).astype(F32)
            middle = (total - high).astype(BF16).astype(F32)
            low = total - high - middle
            line = iota((16, HEAD_DIM), 0)
            log_rows = jnp.where(line == 0, high, jnp.where(line == 1, middle, low)).astype(BF16)
            for p in range(per_head):
                j = h * per_head + p
                state_out[j, 0:rows, :] = state[p * rows : (p + 1) * rows].astype(BF16)
                state_out[j, rows : rows + 16, :] = log_rows

    pl.semaphore_wait(barrier, partners)

    far_first = sorted(range(1, n_ctx), key=lambda d: -min(d, n_ctx - d))

    def z_copy(phase, d, out, into, theirs):
        peer = (ctx + d) % n_ctx
        return remote(
            out.at[peer], into.at[theirs], z_send.at[phase, d], z_recv.at[phase, d], ctx=peer
        )

    if n_ctx > 1:
        for d in far_first:
            z_copy(0, d, state_out, state_in, ctx).start()
    def columns(i):
        return pl.ds(pl.multiple_of(i * cols, 128), cols)

    def pair_w(i):
        return remote(
            w_hbm.at[:, columns(i)],
            weights.at[1, :, columns(i)],
            pair_send.at[i],
            pair_recv.at[i],
            exp=exp_at(0, 1),
        )

    for i in range(chunks):
        pair_w(i).start()
    if n_ctx > 1:
        state_in[ctx] = state_out[ctx]

    loads[3].wait()
    causal = iota((length, length), 0) >= iota((length, length), 1)
    for h in range(HEAD_DEV):
        at = slice(h * HEAD_DIM, (h + 1) * HEAD_DIM)
        scores = contract(q_ref[:, at], k_ref[:, at], ((1,), (1,)))
        gap = b_col[:, h : h + 1] - b_row[h : h + 1, :]
        mix = jnp.where(causal, scores * jnp.exp(jnp.minimum(gap, 0.0)), 0.0).astype(BF16)
        inner[:, at] = jnp.dot(mix, v_ref[:, at], preferred_element_type=F32)

    loads[4].wait()
    ids = ids_ref[...]
    experts = iota((n_exp, tok), 0)
    is_first = (ids[0:1] == experts).astype(F32)
    match = is_first + (ids[1:2] == experts).astype(F32)
    earlier = (iota((tok, tok), 0) < iota((tok, tok), 1)).astype(BF16)
    rank = jnp.dot(match.astype(BF16), earlier, preferred_element_type=F32)
    code = jnp.where(match > 0.5, rank, -1.0).astype(BF16)
    slot_rows = n_exp * 8
    spread = (iota((slot_rows, n_exp), 0) // 8 == iota((slot_rows, n_exp), 1)).astype(BF16)
    codes = jnp.dot(spread, code, preferred_element_type=F32)
    line = iota((slot_rows, tok), 0) % 8
    picks[...] = (codes == line.astype(F32)).astype(BF16)

    if n_ctx > 1:
        for d in far_first:
            z_copy(0, d, state_out, state_in, (ctx - d + n_ctx) % n_ctx).wait_recv()
        carried = jnp.zeros((rows, HEAD_DIM), F32)
        for n in range(n_ctx):
            scan_out[n] = carried.astype(BF16)
            if n < n_ctx - 1:
                logs = state_in[n, rows : rows + 16, :].astype(F32)
                total = logs[0:1] + logs[1:2] + logs[2:3]
                carried = jnp.exp(total) * carried + state_in[n, 0:rows, :].astype(F32)
        for d in far_first:
            z_copy(1, d, scan_out, scan_in, ctx).start()
        scan_in[ctx] = scan_out[ctx]
        for d in far_first:
            z_copy(1, d, scan_out, scan_in, (ctx - d + n_ctx) % n_ctx).wait_recv()

    grow = jnp.exp(b_col)
    for h in range(HEAD_DEV):
        at = slice(h * HEAD_DIM, (h + 1) * HEAD_DIM)
        whole = inner[:, at]
        if n_ctx > 1:
            pieces = [scan_in[h * per_head + p] for p in range(per_head)]
            incoming = jnp.concatenate(pieces, axis=0) if per_head > 1 else pieces[0]
            carried = jnp.dot(q_ref[:, at], incoming, preferred_element_type=F32)
            whole = whole + grow[:, h : h + 1] * carried
        split = whole.astype(BF16).reshape(n_y, 2, tok, HEAD_DIM)
        for c in range(2):
            attended[c, :, at] = split[:, c].reshape(n_y * tok, HEAD_DIM)
    pair_a = remote(
        attended.at[1 - core], att_in, pair_send.at[chunks], pair_recv.at[chunks], exp=exp_at(0, 1)
    )
    pair_a.start()
    loads[5].wait()
    loads[6].wait()

    right, left = exp_at(1), exp_at(-1)
    span = cols // 2

    def ring_copy(way, step, i):
        return remote(
            ring_out.at[way, step, i],
            ring_in.at[way, step, i],
            ring_send.at[way, step, i],
            ring_recv.at[way, step, i],
            exp=left if way else right,
        )

    def half_copy(way, step, i, p):
        part = pl.ds(p * span, span)
        return remote(
            ring_out.at[way, step, i, :, part],
            ring_in.at[way, step, i, :, part],
            half_send.at[way, step, i, p],
            half_recv.at[way, step, i, p],
            exp=left if way else right,
        )

    def arrived(way, step, i):
        if step > 1:
            ring_copy(way, step, i).wait_recv()
        else:
            for p in range(2):
                if step == 1 or p == way:
                    half_copy(way, step, i, p).wait_recv()

    def dest(way, step):
        away = half - step
        return (y - away + n_y) % n_y if way else (y + away) % n_y

    def first_send(way, step, i, p):
        part = slice(p * span, (p + 1) * span)
        ring_out[way, step, i, :, part] = prod[i, dest(way, step), :, part].astype(BF16)
        half_copy(way, step, i, p).start()

    def pass_on(step, i):
        for way in range(2):
            arrived(way, step - 1, i)
            total = prod[i, dest(way, step)] + ring_in[way, step - 1, i].astype(F32)
            ring_out[way, step, i] = total.astype(BF16)
            ring_copy(way, step, i).start()

    lag = 2 if half > 1 else 0

    @pl.loop(0, chunks + lag)
    def _(i):
        @pl.when(i < chunks)
        def _():
            at = columns(i)
            term = jnp.dot(attended[core], weights[0, :, at], preferred_element_type=F32)

            @pl.when(i == 0)
            def _():
                pair_a.wait_recv()

            pair_w(i).wait_recv()
            term = term + jnp.dot(att_in[...], weights[1, :, at], preferred_element_type=F32)
            prod[i] = term.reshape(n_y, tok, cols)
            for way in range(2):
                first_send(way, 0, i, way)
            if half > 1:
                for way in range(2):
                    first_send(way, 1, i, 1 - way)

        if half > 1:

            @pl.when(i >= lag)
            def _():
                now = i - lag
                for way in range(2):
                    part = slice(way * span, (way + 1) * span)
                    half_copy(way, 0, now, way).wait_recv()
                    total = prod[now, dest(way, 1), :, part]
                    total = total + ring_in[way, 0, now, :, part].astype(F32)
                    ring_out[way, 1, now, :, part] = total.astype(BF16)
                    half_copy(way, 1, now, way).start()

    for step in range(2, half):

        @pl.loop(0, chunks)
        def _(i, step=step):
            pass_on(step, i)

    def shift_copy(i):
        return remote(
            shift_out.at[i],
            shift_in.at[i],
            shift_send.at[i],
            shift_recv.at[i],
            section=(sec + 1) % n_sec,
        )

    def slot_copy(i, dy, flip, sender):
        peer = exp_at(dy, flip)
        k = dy * 2 + flip
        return remote(
            placed.at[i, peer],
            rows_out.at[sender, :, columns(i)],
            slot_send.at[i, k],
            slot_recv.at[i, k],
            exp=peer,
        )

    def own_copy(i):
        return pltpu.make_async_copy(
            placed.at[i, exp], rows_out.at[exp, :, columns(i)], own_sem.at[i]
        )

    order = sorted(range(1, n_y), key=lambda d: -min(d, n_y - d)) + [0]
    others = [(dy, flip) for dy in order for flip in (0, 1) if (dy, flip) != (0, 0)]

    def place(i):
        slots = jnp.dot(picks[...], shift_in[i], preferred_element_type=F32)
        placed[i] = slots.reshape(n_exp, 8, cols)[:, 0:CAP].astype(BF16)
        for dy, flip in others:
            slot_copy(i, dy, flip, exp).start()
        own_copy(i).start()

    squares[...] = jnp.zeros_like(squares)

    def add_squares(i):
        if n_sec > 1:
            shift_copy(i).wait_recv()
        wide = shift_in[i].astype(F32)
        squares[...] += jnp.sum(wide * wide, axis=-1, keepdims=True)

    @pl.loop(0, chunks)
    def _(i):
        arrived(0, half - 1, i)
        arrived(1, half - 1, i)
        at = columns(i)
        for p in range(2):
            part = slice(p * span, (p + 1) * span)
            total = prod[i, y, :, part]
            for way in range(2):
                if half > 1 or way == p:
                    total = total + ring_in[way, half - 1, i, :, part].astype(F32)
            wide = res_ref[:, pl.ds(pl.multiple_of(i * cols + p * span, 128), span)]
            shift_out[i, :, part] = (total + wide.astype(F32)).astype(BF16)
        if n_sec > 1:
            shift_copy(i).start()
        else:
            shift_in[i] = shift_out[i]

        @pl.when(jnp.logical_and(i >= 2, i < RAW + 2))
        def _():
            now = i - 2
            add_squares(now)
            place(now)

    @pl.loop(RAW, chunks)
    def _(i):
        add_squares(i)

    loads[7].wait()
    loads[8].wait()
    factor = lax.rsqrt(squares[:, 0:1] / width + EPS)
    logits = jnp.zeros((n_exp, tok), F32)
    for i in range(chunks):
        at = slice(i * cols, (i + 1) * cols)
        normed = (shift_in[i].astype(F32) * factor * gain_ref[:, at]).astype(BF16)
        if i >= RAW:
            shift_in[i] = normed
        logits = logits + contract(router_ref[:, at], normed, ((1,), (1,)))
    picked0 = jnp.sum(logits * is_first, axis=0, keepdims=True)
    picked1 = jnp.sum(logits * (match - is_first), axis=0, keepdims=True)
    gate0 = 1.0 / (1.0 + jnp.exp(picked1 - picked0))
    gate1 = 1.0 - gate0
    diagonal = (iota((tok, tok), 0) == iota((tok, tok), 1)).astype(F32)
    lying = jnp.sum(diagonal * factor, axis=0, keepdims=True)
    first8 = jnp.dot(spread, is_first.astype(BF16), preferred_element_type=F32)
    info = jnp.where(line < CAP, lying, jnp.where(first8 > 0.5, gate0, gate1))
    info = jnp.where(codes == (line % CAP).astype(F32), info, 0.0)
    info = jnp.sum(info, axis=-1, keepdims=True)
    meta_out[...] = jnp.broadcast_to(info, (slot_rows, 128)).reshape(n_exp, 8, 128)

    def meta_copy(dy, flip, sender):
        peer = exp_at(dy, flip)
        k = dy * 2 + flip
        return remote(
            meta_out.at[peer], meta_in.at[sender], meta_send.at[k], meta_recv.at[k], exp=peer
        )

    for dy, flip in others:
        meta_copy(dy, flip, exp).start()
    own_meta = pltpu.make_async_copy(meta_out.at[exp], meta_in.at[exp], own_sem.at[chunks])
    own_meta.start()

    @pl.loop(RAW, chunks)
    def _(i):
        place(i)

    pair_a.wait_send()
    for d in far_first:
        for phase, (out, into) in enumerate(((state_out, state_in), (scan_out, scan_in))):
            z_copy(phase, d, out, into, ctx).wait_send()

    @pl.loop(0, chunks)
    def _(i):
        pair_w(i).wait_send()
        for way in range(2):
            for step in range(half):
                if step > 1:
                    ring_copy(way, step, i).wait_send()
                else:
                    for p in range(2):
                        if step == 1 or p == way:
                            half_copy(way, step, i, p).wait_send()
        if n_sec > 1:
            shift_copy(i).wait_send()
        own_copy(i).wait()
        for dy, flip in others:
            slot_copy(i, dy, flip, exp).wait_send()
            slot_copy(i, dy, flip, exp_at(-dy, flip)).wait_recv()

    own_meta.wait()
    for dy, flip in others:
        meta_copy(dy, flip, exp).wait_send()
        meta_copy(dy, flip, exp_at(-dy, flip)).wait_recv()


def finish(rows_in, meta, gain, rows_out, gates_out, scaled, sem):
    n_exp, _, width = rows_in.shape
    head = RAW * COLS
    rest = pltpu.make_async_copy(
        rows_in.at[:, :, head:width], rows_out.at[:, :, head:width], sem.at[0]
    )
    rest.start()
    wide = rows_in[:, :, 0:head].astype(F32) * meta[:, 0:CAP, 0:1]
    scaled[...] = (wide * gain[:, 0:head].reshape(1, 1, head)).astype(BF16)
    first = pltpu.make_async_copy(scaled, rows_out.at[:, :, 0:head], sem.at[1])
    first.start()
    lane = iota((CAP, n_exp), 1)
    gates = jnp.zeros((CAP, n_exp), F32)
    for j in range(n_exp):
        gates = jnp.where(lane == j, meta[j, CAP : 2 * CAP, 0:n_exp], gates)
    gates_out[...] = gates.astype(BF16)
    rest.wait()
    first.wait()


def on_device(
    sizes, queries, keys_in, values, decay_rate, out_weight, residual, norm_gain, router, expert_ids
):
    n_sec, n_ctx, n_exp = sizes
    length, inner_width = queries.shape[1:]
    width = out_weight.shape[-1]
    tok = residual.shape[1]
    n_y = n_exp // 2
    half = n_y // 2
    cols = COLS
    chunks = width // cols
    rows = HEAD_DEV * HEAD_DIM // n_ctx
    any_space = pl.BlockSpec(memory_space=pl.ANY)
    dma = pltpu.SemaphoreType.DMA
    vmem_space = pl.BlockSpec(memory_space=pltpu.VMEM)
    slots, meta = pl.pallas_call(
        functools.partial(kernel, (n_sec, n_ctx, n_exp, length, width, cols)),
        out_shape=(
            jax.ShapeDtypeStruct((n_exp, CAP, width), BF16),
            jax.ShapeDtypeStruct((n_exp, 8, 128), F32),
        ),
        in_specs=[pl.BlockSpec(memory_space=pltpu.HBM)] * 9,
        out_specs=(any_space, any_space),
        scratch_shapes=[
            pltpu.VMEM((length, inner_width), BF16),
            pltpu.VMEM((length, inner_width), BF16),
            pltpu.VMEM((length, inner_width), BF16),
            pltpu.VMEM((HEAD_DEV, length), F32),
            pltpu.VMEM((tok, width), BF16),
            pltpu.VMEM((1, width), F32),
            pltpu.VMEM((n_exp, width), BF16),
            pltpu.VMEM((2, tok), jnp.int32),
            pltpu.VMEM((2, inner_width, width), BF16),
            pltpu.VMEM((length, inner_width), F32),
            pltpu.VMEM((2, n_y * tok, inner_width), BF16),
            pltpu.VMEM((n_y * tok, inner_width), BF16),
            pltpu.VMEM((chunks, n_y, tok, cols), F32),
            pltpu.VMEM((n_ctx, rows + 16, HEAD_DIM), BF16),
            pltpu.VMEM((n_ctx, rows + 16, HEAD_DIM), BF16),
            pltpu.VMEM((n_ctx, rows, HEAD_DIM), BF16),
            pltpu.VMEM((n_ctx, rows, HEAD_DIM), BF16),
            pltpu.VMEM((2, half, chunks, tok, cols), BF16),
            pltpu.VMEM((2, half, chunks, tok, cols), BF16),
            pltpu.VMEM((chunks, tok, cols), BF16),
            pltpu.VMEM((chunks, tok, cols), BF16),
            pltpu.VMEM((chunks, n_exp, CAP, cols), BF16),
            pltpu.VMEM((n_exp * 8, tok), BF16),
            pltpu.VMEM((tok, 128), F32),
            pltpu.VMEM((n_exp, 8, 128), F32),
            dma((9,)),
            dma((chunks + 1,)),
            dma((chunks + 1,)),
            dma((2, n_ctx)),
            dma((2, n_ctx)),
            dma((2, half, chunks)),
            dma((2, half, chunks)),
            dma((2, 2, chunks, 2)),
            dma((2, 2, chunks, 2)),
            dma((chunks,)),
            dma((chunks,)),
            dma((chunks, n_exp)),
            dma((chunks, n_exp)),
            dma((n_exp,)),
            dma((n_exp,)),
            dma((chunks + 1,)),
        ],
        compiler_params=pltpu.CompilerParams(
            collective_id=0, has_side_effects=True, vmem_limit_bytes=VMEM_MIB * 2**20
        ),
    )(
        *(
            pltpu.with_memory_space_constraint(x, pltpu.HBM)
            for x in (
                queries[0],
                keys_in[0],
                values[0],
                decay_rate[0],
                out_weight[0],
                residual[0],
                norm_gain,
                router[0].T,
                expert_ids[0].T,
            )
        )
    )
    rows_out, gates = pl.pallas_call(
        finish,
        out_shape=(
            jax.ShapeDtypeStruct((n_exp, CAP, width), BF16),
            jax.ShapeDtypeStruct((CAP, n_exp), BF16),
        ),
        in_specs=[vmem_space] * 3,
        out_specs=(any_space, vmem_space),
        scratch_shapes=[pltpu.VMEM((n_exp, CAP, RAW * cols), BF16), dma((2,))],
        compiler_params=pltpu.CompilerParams(vmem_limit_bytes=8 * 2**20),
    )(slots, meta, norm_gain)
    return (rows_out[None, None, None], gates.T[None, None, None])


def solution(mesh):
    sizes = tuple(mesh.shape[a] for a in ("section", "ctx", "exp"))
    placed = (
        P("section", "ctx", "exp"),
        P("section", "ctx", "exp"),
        P("section", "ctx", "exp"),
        P("section", "exp", "ctx"),
        P("section", "exp", None),
        P("section", ("ctx", "exp"), None),
        P("section", None),
        P("section", None, None),
        P("section", ("ctx", "exp"), None),
    )
    return jax.shard_map(
        functools.partial(on_device, sizes),
        mesh=mesh,
        in_specs=placed,
        out_specs=(
            P("section", "ctx", "exp", None, None, None),
            P("section", "ctx", "exp", None, None),
        ),
        check_vma=False,
    )
```

```python
import functools

import jax
import jax.numpy as jnp
from jax import lax
from jax.experimental import pallas as pl
from jax.experimental.pallas import tpu as pltpu
from jax.sharding import PartitionSpec as P

HEAD_DIM = 128
HEAD_DEV = 4
CAP = 4
EPS = 1e-05
COLS = 1536
RAW = 1
VMEM_MIB = 36
MESH = pl.DeviceIdType.MESH
F32 = jnp.float32
BF16 = jnp.bfloat16


def iota(shape, dim):
    return lax.broadcasted_iota(jnp.int32, shape, dim)


def remote(src, dst, send_sem, recv_sem, **device):
    return pltpu.make_async_remote_copy(
        src_ref=src,
        dst_ref=dst,
        send_sem=send_sem,
        recv_sem=recv_sem,
        device_id=device,
        device_id_type=MESH,
    )


def contract(a, b, dims, **kw):
    return lax.dot_general(a, b, (dims, ((), ())), preferred_element_type=F32, **kw)


def kernel(
    sizes,
    q_hbm,
    k_hbm,
    v_hbm,
    decay_hbm,
    w_hbm,
    res_hbm,
    gain_hbm,
    router_hbm,
    ids_hbm,
    rows_out,
    meta_in,
    q_ref,
    k_ref,
    v_ref,
    decay_ref,
    res_ref,
    gain_ref,
    router_ref,
    ids_ref,
    weights,
    inner,
    attended,
    att_in,
    prod,
    state_out,
    state_in,
    scan_out,
    scan_in,
    ring_out,
    ring_in,
    shift_out,
    shift_in,
    placed,
    picks,
    squares,
    meta_out,
    load_sem,
    pair_send,
    pair_recv,
    z_send,
    z_recv,
    ring_send,
    ring_recv,
    shift_send,
    shift_recv,
    slot_send,
    slot_recv,
    meta_send,
    meta_recv,
    own_sem,
):
    n_sec, n_ctx, n_exp, length, width, cols = sizes
    n_y = n_exp // 2
    half = n_y // 2
    chunks = width // cols
    tok = length // n_exp
    sec = lax.axis_index("section")
    ctx = lax.axis_index("ctx")
    exp = lax.axis_index("exp")
    y = exp // 2
    core = exp % 2

    def exp_at(dy, flip=0):
        there = (y + dy + n_y) % n_y
        side = 1 - core if flip else core
        return there * 2 + side

    loads = [
        pltpu.make_async_copy(src, dst, load_sem.at[i])
        for i, (src, dst) in enumerate(
            (
                (decay_hbm, decay_ref),
                (k_hbm, k_ref),
                (v_hbm, v_ref),
                (q_hbm, q_ref),
                (ids_hbm, ids_ref),
                (w_hbm, weights.at[0]),
                (res_hbm, res_ref),
                (gain_hbm, gain_ref),
                (router_hbm, router_ref),
            )
        )
    ]
    for load in loads:
        load.start()

    barrier = pltpu.get_barrier_semaphore()
    partners = 0
    for d in range(1, n_exp):
        pl.semaphore_signal(
            barrier, inc=1, device_id={"exp": (exp + d) % n_exp}, device_id_type=MESH
        )
        partners += 1
    for d in range(1, n_ctx):
        pl.semaphore_signal(
            barrier, inc=1, device_id={"ctx": (ctx + d) % n_ctx}, device_id_type=MESH
        )
        partners += 1
    if n_sec > 1:
        for d in (1, n_sec - 1):
            pl.semaphore_signal(
                barrier, inc=1, device_id={"section": (sec + d) % n_sec}, device_id_type=MESH
            )
            partners += 1

    loads[0].wait()
    lower = (iota((length, length), 0) >= iota((length, length), 1)).astype(BF16)
    rest = -decay_ref[...]
    b_col = jnp.zeros((length, HEAD_DEV), F32)
    b_row = jnp.zeros((HEAD_DEV, length), F32)
    for _ in range(3):
        part = rest.astype(BF16)
        rest = rest - part.astype(F32)
        b_col = b_col + contract(lower, part, ((1,), (1,)))
        b_row = b_row + contract(part, lower, ((1,), (1,)))
    b_last = b_col[length - 1 :, :]
    tail = jnp.exp(b_last - b_col)
    loads[1].wait()
    loads[2].wait()
    rows = HEAD_DEV * HEAD_DIM // n_ctx
    per_head = max(HEAD_DIM // rows, 1)
    for h in range(HEAD_DEV):
        at = slice(h * HEAD_DIM, (h + 1) * HEAD_DIM)
        keyed = (k_ref[:, at].astype(F32) * tail[:, h : h + 1]).astype(BF16)
        state = contract(keyed, v_ref[:, at], ((0,), (0,)))
        if n_ctx > 1:
            total = jnp.broadcast_to(b_last[:, h : h + 1], (16, HEAD_DIM))
            high = total.astype(BF16).astype(F32)
            middle = (total - high).astype(BF16).astype(F32)
            low = total - high - middle
            line = iota((16, HEAD_DIM), 0)
            log_rows = jnp.where(line == 0, high, jnp.where(line == 1, middle, low)).astype(BF16)
            for p in range(per_head):
                j = h * per_head + p
                state_out[j, 0:rows, :] = state[p * rows : (p + 1) * rows].astype(BF16)
                state_out[j, rows : rows + 16, :] = log_rows

    pl.semaphore_wait(barrier, partners)

    far_first = sorted(range(1, n_ctx), key=lambda d: -min(d, n_ctx - d))

    def z_copy(phase, d, out, into, theirs):
        peer = (ctx + d) % n_ctx
        return remote(
            out.at[peer], into.at[theirs], z_send.at[phase], z_recv.at[phase], ctx=peer
        )

    def z_all(phase, out, into):
        span = pl.ds(0, n_ctx - 1)
        return remote(
            out.at[span], into.at[span], z_send.at[phase], z_recv.at[phase], ctx=(ctx + 1) % n_ctx
        )

    if n_ctx > 1:
        for d in far_first:
            z_copy(0, d, state_out, state_in, ctx).start()
    def columns(i):
        return pl.ds(pl.multiple_of(i * cols, 128), cols)

    def pair_w(i):
        return remote(
            w_hbm.at[:, columns(i)],
            weights.at[1, :, columns(i)],
            pair_send.at[0],
            pair_recv.at[i],
            exp=exp_at(0, 1),
        )

    for i in range(chunks):
        pair_w(i).start()
    if n_ctx > 1:
        state_in[ctx] = state_out[ctx]

    loads[3].wait()
    causal = iota((length, length), 0) >= iota((length, length), 1)
    for h in range(HEAD_DEV):
        at = slice(h * HEAD_DIM, (h + 1) * HEAD_DIM)
        scores = contract(q_ref[:, at], k_ref[:, at], ((1,), (1,)))
        gap = b_col[:, h : h + 1] - b_row[h : h + 1, :]
        mix = jnp.where(causal, scores * jnp.exp(jnp.minimum(gap, 0.0)), 0.0).astype(BF16)
        inner[:, at] = jnp.dot(mix, v_ref[:, at], preferred_element_type=F32)

    loads[4].wait()
    ids = ids_ref[...]
    experts = iota((n_exp, tok), 0)
    is_first = (ids[0:1] == experts).astype(F32)
    match = is_first + (ids[1:2] == experts).astype(F32)
    earlier = (iota((tok, tok), 0) < iota((tok, tok), 1)).astype(BF16)
    rank = jnp.dot(match.astype(BF16), earlier, preferred_element_type=F32)
    code = jnp.where(match > 0.5, rank, -1.0).astype(BF16)
    slot_rows = n_exp * 8
    spread = (iota((slot_rows, n_exp), 0) // 8 == iota((slot_rows, n_exp), 1)).astype(BF16)
    codes = jnp.dot(spread, code, preferred_element_type=F32)
    line = iota((slot_rows, tok), 0) % 8
    picks[...] = (codes == line.astype(F32)).astype(BF16)

    if n_ctx > 1:
        z_all(0, state_out, state_in).wait_recv()
        carried = jnp.zeros((rows, HEAD_DIM), F32)
        for n in range(n_ctx):
            scan_out[n] = carried.astype(BF16)
            if n < n_ctx - 1:
                logs = state_in[n, rows : rows + 16, :].astype(F32)
                total = logs[0:1] + logs[1:2] + logs[2:3]
                carried = jnp.exp(total) * carried + state_in[n, 0:rows, :].astype(F32)
        for d in far_first:
            z_copy(1, d, scan_out, scan_in, ctx).start()
        scan_in[ctx] = scan_out[ctx]
        z_all(1, scan_out, scan_in).wait_recv()

    grow = jnp.exp(b_col)
    for h in range(HEAD_DEV):
        at = slice(h * HEAD_DIM, (h + 1) * HEAD_DIM)
        whole = inner[:, at]
        if n_ctx > 1:
            pieces = [scan_in[h * per_head + p] for p in range(per_head)]
            incoming = jnp.concatenate(pieces, axis=0) if per_head > 1 else pieces[0]
            carried = jnp.dot(q_ref[:, at], incoming, preferred_element_type=F32)
            whole = whole + grow[:, h : h + 1] * carried
        split = whole.astype(BF16).reshape(n_y, 2, tok, HEAD_DIM)
        for c in range(2):
            attended[c, :, at] = split[:, c].reshape(n_y * tok, HEAD_DIM)
    pair_a = remote(
        attended.at[1 - core], att_in, pair_send.at[1], pair_recv.at[chunks], exp=exp_at(0, 1)
    )
    pair_a.start()
    loads[5].wait()
    loads[6].wait()

    right, left = exp_at(1), exp_at(-1)
    span = cols // 2

    def ring_copy(way, step, i):
        return remote(
            ring_out.at[way, step, i],
            ring_in.at[way, step, i],
            ring_send.at[2],
            ring_recv.at[way, step, i],
            exp=left if way else right,
        )

    def half_copy(way, step, i, p):
        part = pl.ds(p * span, span)
        return remote(
            ring_out.at[way, step, i, :, part],
            ring_in.at[way, step, i, :, part],
            ring_send.at[step],
            ring_recv.at[way, step, i],
            exp=left if way else right,
        )

    def arrived(way, step, i):
        if step > 0:
            ring_copy(way, step, i).wait_recv()
        else:
            half_copy(way, 0, i, way).wait_recv()

    def dest(way, step):
        away = half - step
        return (y - away + n_y) % n_y if way else (y + away) % n_y

    def first_send(way, step, i, p):
        part = slice(p * span, (p + 1) * span)
        ring_out[way, step, i, :, part] = prod[i, dest(way, step), :, part].astype(BF16)
        half_copy(way, step, i, p).start()

    def pass_on(step, i):
        for way in range(2):
            arrived(way, step - 1, i)
            total = prod[i, dest(way, step)] + ring_in[way, step - 1, i].astype(F32)
            ring_out[way, step, i] = total.astype(BF16)
            ring_copy(way, step, i).start()

    lag = 2 if half > 1 else 0

    @pl.loop(0, chunks + lag)
    def _(i):
        @pl.when(i < chunks)
        def _():
            at = columns(i)
            term = jnp.dot(attended[core], weights[0, :, at], preferred_element_type=F32)

            @pl.when(i == 0)
            def _():
                pair_a.wait_recv()

            pair_w(i).wait_recv()
            term = term + jnp.dot(att_in[...], weights[1, :, at], preferred_element_type=F32)
            prod[i] = term.reshape(n_y, tok, cols)
            for way in range(2):
                first_send(way, 0, i, way)
            if half > 1:
                for way in range(2):
                    first_send(way, 1, i, 1 - way)

        if half > 1:

            @pl.when(i >= lag)
            def _():
                now = i - lag
                for way in range(2):
                    part = slice(way * span, (way + 1) * span)
                    half_copy(way, 0, now, way).wait_recv()
                    total = prod[now, dest(way, 1), :, part]
                    total = total + ring_in[way, 0, now, :, part].astype(F32)
                    ring_out[way, 1, now, :, part] = total.astype(BF16)
                    half_copy(way, 1, now, way).start()

    for step in range(2, half):

        @pl.loop(0, chunks)
        def _(i, step=step):
            pass_on(step, i)

    def shift_copy(i):
        return remote(
            shift_out.at[i],
            shift_in.at[i],
            shift_send.at[0],
            shift_recv.at[i],
            section=(sec + 1) % n_sec,
        )

    groups = (pl.ds(0, RAW * cols), pl.ds(RAW * cols, width - RAW * cols))

    def slot_copy(g, dy, flip):
        peer = exp_at(dy, flip)
        return remote(
            placed.at[peer, :, groups[g]],
            rows_out.at[exp, :, groups[g]],
            slot_send.at[g],
            slot_recv.at[g],
            exp=peer,
        )

    def own_copy(g):
        return pltpu.make_async_copy(
            placed.at[exp, :, groups[g]], rows_out.at[exp, :, groups[g]], own_sem.at[g]
        )

    order = sorted(range(1, n_y), key=lambda d: -min(d, n_y - d)) + [0]
    others = [(dy, flip) for dy in order for flip in (0, 1) if (dy, flip) != (0, 0)]

    def place(i):
        slots = jnp.dot(picks[...], shift_in[i], preferred_element_type=F32)
        placed[:, :, columns(i)] = slots.reshape(n_exp, 8, cols)[:, 0:CAP].astype(BF16)

    def send_slots(g):
        for dy, flip in others:
            slot_copy(g, dy, flip).start()
        own_copy(g).start()

    squares[...] = jnp.zeros_like(squares)

    def add_squares(i):
        if n_sec > 1:
            shift_copy(i).wait_recv()
        wide = shift_in[i].astype(F32)
        squares[...] += jnp.sum(wide * wide, axis=-1, keepdims=True)

    @pl.loop(0, chunks)
    def _(i):
        arrived(0, half - 1, i)
        arrived(1, half - 1, i)
        at = columns(i)
        for p in range(2):
            part = slice(p * span, (p + 1) * span)
            total = prod[i, y, :, part]
            for way in range(2):
                if half > 1 or way == p:
                    total = total + ring_in[way, half - 1, i, :, part].astype(F32)
            wide = res_ref[:, pl.ds(pl.multiple_of(i * cols + p * span, 128), span)]
            shift_out[i, :, part] = (total + wide.astype(F32)).astype(BF16)
        if n_sec > 1:
            shift_copy(i).start()
        else:
            shift_in[i] = shift_out[i]

        @pl.when(jnp.logical_and(i >= 2, i < RAW + 2))
        def _():
            now = i - 2
            add_squares(now)
            place(now)

            @pl.when(now == RAW - 1)
            def _():
                send_slots(0)

    @pl.loop(RAW, chunks)
    def _(i):
        add_squares(i)

    loads[7].wait()
    loads[8].wait()
    factor = lax.rsqrt(squares[:, 0:1] / width + EPS)
    logits = jnp.zeros((n_exp, tok), F32)
    for i in range(chunks):
        at = slice(i * cols, (i + 1) * cols)
        normed = (shift_in[i].astype(F32) * factor * gain_ref[:, at]).astype(BF16)
        if i >= RAW:
            shift_in[i] = normed
        logits = logits + contract(router_ref[:, at], normed, ((1,), (1,)))
    picked0 = jnp.sum(logits * is_first, axis=0, keepdims=True)
    picked1 = jnp.sum(logits * (match - is_first), axis=0, keepdims=True)
    gate0 = 1.0 / (1.0 + jnp.exp(picked1 - picked0))
    gate1 = 1.0 - gate0
    diagonal = (iota((tok, tok), 0) == iota((tok, tok), 1)).astype(F32)
    lying = jnp.sum(diagonal * factor, axis=0, keepdims=True)
    first8 = jnp.dot(spread, is_first.astype(BF16), preferred_element_type=F32)
    info = jnp.where(line < CAP, lying, jnp.where(first8 > 0.5, gate0, gate1))
    info = jnp.where(codes == (line % CAP).astype(F32), info, 0.0)
    info = jnp.sum(info, axis=-1, keepdims=True)
    meta_out[...] = jnp.broadcast_to(info, (slot_rows, 128)).reshape(n_exp, 8, 128)

    for dy, flip in others:
        peer = exp_at(dy, flip)
        remote(
            meta_out.at[peer], meta_in.at[exp], meta_send.at[0], meta_recv.at[0], exp=peer
        ).start()
    own_meta = pltpu.make_async_copy(meta_out.at[exp], meta_in.at[exp], own_sem.at[2])
    own_meta.start()

    @pl.loop(RAW, chunks)
    def _(i):
        place(i)

    send_slots(1)

    pair_a.wait_send()
    remote(
        w_hbm, weights.at[1], pair_send.at[0], pair_recv.at[0], exp=exp_at(0, 1)
    ).wait_send()
    if n_ctx > 1:
        z_all(0, state_out, state_in).wait_send()
        z_all(1, scan_out, scan_in).wait_send()

    for step in range(min(half, 2)):
        sent = ring_out.at[0, 0] if step == 0 else ring_out.at[:, 1]
        into = ring_in.at[0, 0] if step == 0 else ring_in.at[:, 1]
        remote(sent, into, ring_send.at[step], ring_recv.at[0, 0, 0], exp=right).wait_send()
    if half > 2:
        later = pl.ds(2, half - 2)
        remote(
            ring_out.at[:, later],
            ring_in.at[:, later],
            ring_send.at[2],
            ring_recv.at[0, 0, 0],
            exp=right,
        ).wait_send()
    if n_sec > 1:
        remote(
            shift_out, shift_in, shift_send.at[0], shift_recv.at[0], section=(sec + 1) % n_sec
        ).wait_send()
    own_meta.wait()
    meta_all = remote(
        meta_out.at[pl.ds(0, n_exp - 1)],
        meta_in.at[pl.ds(0, n_exp - 1)],
        meta_send.at[0],
        meta_recv.at[0],
        exp=right,
    )
    meta_all.wait_send()
    meta_all.wait_recv()
    for g in range(2):
        own_copy(g).wait()
        most = pl.ds(0, n_exp - 1)
        slots_all = remote(
            placed.at[most, :, groups[g]],
            rows_out.at[most, :, groups[g]],
            slot_send.at[g],
            slot_recv.at[g],
            exp=right,
        )
        slots_all.wait_send()
        slots_all.wait_recv()


def finish(rows_in, meta, gain, rows_out, gates_out, scaled, sem):
    n_exp, _, width = rows_in.shape
    head = RAW * COLS
    rest = pltpu.make_async_copy(
        rows_in.at[:, :, head:width], rows_out.at[:, :, head:width], sem.at[0]
    )
    rest.start()
    wide = rows_in[:, :, 0:head].astype(F32) * meta[:, 0:CAP, 0:1]
    scaled[...] = (wide * gain[:, 0:head].reshape(1, 1, head)).astype(BF16)
    first = pltpu.make_async_copy(scaled, rows_out.at[:, :, 0:head], sem.at[1])
    first.start()
    lane = iota((CAP, n_exp), 1)
    gates = jnp.zeros((CAP, n_exp), F32)
    for j in range(n_exp):
        gates = jnp.where(lane == j, meta[j, CAP : 2 * CAP, 0:n_exp], gates)
    gates_out[...] = gates.astype(BF16)
    rest.wait()
    first.wait()


def on_device(
    sizes, queries, keys_in, values, decay_rate, out_weight, residual, norm_gain, router, expert_ids
):
    n_sec, n_ctx, n_exp = sizes
    length, inner_width = queries.shape[1:]
    width = out_weight.shape[-1]
    tok = residual.shape[1]
    n_y = n_exp // 2
    half = n_y // 2
    cols = COLS
    chunks = width // cols
    rows = HEAD_DEV * HEAD_DIM // n_ctx
    any_space = pl.BlockSpec(memory_space=pl.ANY)
    dma = pltpu.SemaphoreType.DMA
    vmem_space = pl.BlockSpec(memory_space=pltpu.VMEM)
    slots, meta = pl.pallas_call(
        functools.partial(kernel, (n_sec, n_ctx, n_exp, length, width, cols)),
        out_shape=(
            jax.ShapeDtypeStruct((n_exp, CAP, width), BF16),
            jax.ShapeDtypeStruct((n_exp, 8, 128), F32),
        ),
        in_specs=[pl.BlockSpec(memory_space=pltpu.HBM)] * 9,
        out_specs=(any_space, any_space),
        scratch_shapes=[
            pltpu.VMEM((length, inner_width), BF16),
            pltpu.VMEM((length, inner_width), BF16),
            pltpu.VMEM((length, inner_width), BF16),
            pltpu.VMEM((HEAD_DEV, length), F32),
            pltpu.VMEM((tok, width), BF16),
            pltpu.VMEM((1, width), F32),
            pltpu.VMEM((n_exp, width), BF16),
            pltpu.VMEM((2, tok), jnp.int32),
            pltpu.VMEM((2, inner_width, width), BF16),
            pltpu.VMEM((length, inner_width), F32),
            pltpu.VMEM((2, n_y * tok, inner_width), BF16),
            pltpu.VMEM((n_y * tok, inner_width), BF16),
            pltpu.VMEM((chunks, n_y, tok, cols), F32),
            pltpu.VMEM((n_ctx, rows + 16, HEAD_DIM), BF16),
            pltpu.VMEM((n_ctx, rows + 16, HEAD_DIM), BF16),
            pltpu.VMEM((n_ctx, rows, HEAD_DIM), BF16),
            pltpu.VMEM((n_ctx, rows, HEAD_DIM), BF16),
            pltpu.VMEM((2, half, chunks, tok, cols), BF16),
            pltpu.VMEM((2, half, chunks, tok, cols), BF16),
            pltpu.VMEM((chunks, tok, cols), BF16),
            pltpu.VMEM((chunks, tok, cols), BF16),
            pltpu.VMEM((n_exp, CAP, width), BF16),
            pltpu.VMEM((n_exp * 8, tok), BF16),
            pltpu.VMEM((tok, 128), F32),
            pltpu.VMEM((n_exp, 8, 128), F32),
            dma((9,)),
            dma((2,)),
            dma((chunks + 1,)),
            dma((2,)),
            dma((2,)),
            dma((3,)),
            dma((2, half, chunks)),
            dma((1,)),
            dma((chunks,)),
            dma((2,)),
            dma((2,)),
            dma((1,)),
            dma((1,)),
            dma((3,)),
        ],
        compiler_params=pltpu.CompilerParams(
            collective_id=0, has_side_effects=True, vmem_limit_bytes=VMEM_MIB * 2**20
        ),
    )(
        *(
            pltpu.with_memory_space_constraint(x, pltpu.HBM)
            for x in (
                queries[0],
                keys_in[0],
                values[0],
                decay_rate[0],
                out_weight[0],
                residual[0],
                norm_gain,
                router[0].T,
                expert_ids[0].T,
            )
        )
    )
    rows_out, gates = pl.pallas_call(
        finish,
        out_shape=(
            jax.ShapeDtypeStruct((n_exp, CAP, width), BF16),
            jax.ShapeDtypeStruct((CAP, n_exp), BF16),
        ),
        in_specs=[vmem_space] * 3,
        out_specs=(any_space, vmem_space),
        scratch_shapes=[pltpu.VMEM((n_exp, CAP, RAW * cols), BF16), dma((2,))],
        compiler_params=pltpu.CompilerParams(vmem_limit_bytes=8 * 2**20),
    )(slots, meta, norm_gain)
    return (rows_out[None, None, None], gates.T[None, None, None])


def solution(mesh):
    sizes = tuple(mesh.shape[a] for a in ("section", "ctx", "exp"))
    placed = (
        P("section", "ctx", "exp"),
        P("section", "ctx", "exp"),
        P("section", "ctx", "exp"),
        P("section", "exp", "ctx"),
        P("section", "exp", None),
        P("section", ("ctx", "exp"), None),
        P("section", None),
        P("section", None, None),
        P("section", ("ctx", "exp"), None),
    )
    return jax.shard_map(
        functools.partial(on_device, sizes),
        mesh=mesh,
        in_specs=placed,
        out_specs=(
            P("section", "ctx", "exp", None, None, None),
            P("section", "ctx", "exp", None, None),
        ),
        check_vma=False,
    )
```

```python
import functools

import jax
import jax.numpy as jnp
from jax import lax
from jax.experimental import pallas as pl
from jax.experimental.pallas import tpu as pltpu
from jax.sharding import PartitionSpec as P

HEAD_DIM = 128
HEAD_DEV = 4
CAP = 4
EPS = 1e-05
COLS = 1536
RAW = 1
VMEM_MIB = 36
MESH = pl.DeviceIdType.MESH
F32 = jnp.float32
BF16 = jnp.bfloat16


def iota(shape, dim):
    return lax.broadcasted_iota(jnp.int32, shape, dim)


def remote(src, dst, send_sem, recv_sem, **device):
    return pltpu.make_async_remote_copy(
        src_ref=src,
        dst_ref=dst,
        send_sem=send_sem,
        recv_sem=recv_sem,
        device_id=device,
        device_id_type=MESH,
    )


def contract(a, b, dims, **kw):
    return lax.dot_general(a, b, (dims, ((), ())), preferred_element_type=F32, **kw)


def kernel(
    sizes,
    q_hbm,
    k_hbm,
    v_hbm,
    decay_hbm,
    w_hbm,
    res_hbm,
    gain_hbm,
    router_hbm,
    ids_hbm,
    rows_out,
    meta_in,
    q_ref,
    k_ref,
    v_ref,
    decay_ref,
    res_ref,
    gain_ref,
    router_ref,
    ids_ref,
    weights,
    inner,
    attended,
    att_in,
    prod,
    state_out,
    state_in,
    scan_out,
    scan_in,
    ring_out,
    ring_in,
    shift_out,
    shift_in,
    placed,
    picks,
    squares,
    meta_out,
    load_sem,
    pair_send,
    pair_recv,
    z_send,
    z_recv,
    ring_send,
    ring_recv,
    shift_send,
    shift_recv,
    slot_send,
    slot_recv,
    meta_send,
    meta_recv,
    own_sem,
):
    n_sec, n_ctx, n_exp, length, width, cols = sizes
    n_y = n_exp // 2
    half = n_y // 2
    chunks = width // cols
    tok = length // n_exp
    sec = lax.axis_index("section")
    ctx = lax.axis_index("ctx")
    exp = lax.axis_index("exp")
    y = exp // 2
    core = exp % 2

    def exp_at(dy, flip=0):
        there = (y + dy + n_y) % n_y
        side = 1 - core if flip else core
        return there * 2 + side

    loads = [
        pltpu.make_async_copy(src, dst, load_sem.at[i])
        for i, (src, dst) in enumerate(
            (
                (decay_hbm, decay_ref),
                (k_hbm, k_ref),
                (v_hbm, v_ref),
                (q_hbm, q_ref),
                (ids_hbm, ids_ref),
                (w_hbm, weights.at[0]),
                (res_hbm, res_ref),
                (gain_hbm, gain_ref),
                (router_hbm, router_ref),
            )
        )
    ]
    for load in loads:
        load.start()

    barrier = pltpu.get_barrier_semaphore()
    partners = 0
    for who in (exp_at(0,1), exp_at(1), exp_at(-1)):
        pl.semaphore_signal(barrier, inc=1, device_id={"exp": who}, device_id_type=MESH)
        partners += 1
    for d in range(1, n_ctx):
        pl.semaphore_signal(
            barrier, inc=1, device_id={"ctx": (ctx + d) % n_ctx}, device_id_type=MESH
        )
        partners += 1
    if n_sec > 1:
        for d in (1, n_sec - 1):
            pl.semaphore_signal(
                barrier, inc=1, device_id={"section": (sec + d) % n_sec}, device_id_type=MESH
            )
            partners += 1

    loads[0].wait()
    lower = (iota((length, length), 0) >= iota((length, length), 1)).astype(BF16)
    rest = -decay_ref[...]
    b_col = jnp.zeros((length, HEAD_DEV), F32)
    b_row = jnp.zeros((HEAD_DEV, length), F32)
    for _ in range(3):
        part = rest.astype(BF16)
        rest = rest - part.astype(F32)
        b_col = b_col + contract(lower, part, ((1,), (1,)))
        b_row = b_row + contract(part, lower, ((1,), (1,)))
    b_last = b_col[length - 1 :, :]
    tail = jnp.exp(b_last - b_col)
    loads[1].wait()
    loads[2].wait()
    rows = HEAD_DEV * HEAD_DIM // n_ctx
    per_head = max(HEAD_DIM // rows, 1)
    for h in range(HEAD_DEV):
        at = slice(h * HEAD_DIM, (h + 1) * HEAD_DIM)
        keyed = (k_ref[:, at].astype(F32) * tail[:, h : h + 1]).astype(BF16)
        state = contract(keyed, v_ref[:, at], ((0,), (0,)))
        if n_ctx > 1:
            total = jnp.broadcast_to(b_last[:, h : h + 1], (16, HEAD_DIM))
            high = total.astype(BF16).astype(F32)
            middle = (total - high).astype(BF16).astype(F32)
            low = total - high - middle
            line = iota((16, HEAD_DIM), 0)
            log_rows = jnp.where(line == 0, high, jnp.where(line == 1, middle, low)).astype(BF16)
            for p in range(per_head):
                j = h * per_head + p
                state_out[j, 0:rows, :] = state[p * rows : (p + 1) * rows].astype(BF16)
                state_out[j, rows : rows + 16, :] = log_rows

    pl.semaphore_wait(barrier, partners)

    far_first = sorted(range(1, n_ctx), key=lambda d: -min(d, n_ctx - d))

    def z_copy(phase, d, out, into, theirs):
        peer = (ctx + d) % n_ctx
        return remote(
            out.at[peer], into.at[theirs], z_send.at[phase], z_recv.at[phase], ctx=peer
        )

    def z_all(phase, out, into):
        span = pl.ds(0, n_ctx - 1)
        return remote(
            out.at[span], into.at[span], z_send.at[phase], z_recv.at[phase], ctx=(ctx + 1) % n_ctx
        )

    if n_ctx > 1:
        for d in far_first:
            z_copy(0, d, state_out, state_in, ctx).start()
    def columns(i):
        return pl.ds(pl.multiple_of(i * cols, 128), cols)

    def pair_w(i):
        return remote(
            w_hbm.at[:, columns(i)],
            weights.at[1, :, columns(i)],
            pair_send.at[0],
            pair_recv.at[i],
            exp=exp_at(0, 1),
        )

    for i in range(chunks):
        pair_w(i).start()
    if n_ctx > 1:
        state_in[ctx] = state_out[ctx]

    loads[3].wait()
    causal = iota((length, length), 0) >= iota((length, length), 1)
    for h in range(HEAD_DEV):
        at = slice(h * HEAD_DIM, (h + 1) * HEAD_DIM)
        scores = contract(q_ref[:, at], k_ref[:, at], ((1,), (1,)))
        gap = b_col[:, h : h + 1] - b_row[h : h + 1, :]
        mix = jnp.where(causal, scores * jnp.exp(jnp.minimum(gap, 0.0)), 0.0).astype(BF16)
        inner[:, at] = jnp.dot(mix, v_ref[:, at], preferred_element_type=F32)

    loads[4].wait()
    ids = ids_ref[...]
    experts = iota((n_exp, tok), 0)
    is_first = (ids[0:1] == experts).astype(F32)
    match = is_first + (ids[1:2] == experts).astype(F32)
    earlier = (iota((tok, tok), 0) < iota((tok, tok), 1)).astype(BF16)
    rank = jnp.dot(match.astype(BF16), earlier, preferred_element_type=F32)
    code = jnp.where(match > 0.5, rank, -1.0).astype(BF16)
    slot_rows = n_exp * 8
    spread = (iota((slot_rows, n_exp), 0) // 8 == iota((slot_rows, n_exp), 1)).astype(BF16)
    codes = jnp.dot(spread, code, preferred_element_type=F32)
    line = iota((slot_rows, tok), 0) % 8
    picks[...] = (codes == line.astype(F32)).astype(BF16)

    if n_ctx > 1:
        z_all(0, state_out, state_in).wait_recv()
        carried = jnp.zeros((rows, HEAD_DIM), F32)
        for n in range(n_ctx):
            scan_out[n] = carried.astype(BF16)
            if n < n_ctx - 1:
                logs = state_in[n, rows : rows + 16, :].astype(F32)
                total = logs[0:1] + logs[1:2] + logs[2:3]
                carried = jnp.exp(total) * carried + state_in[n, 0:rows, :].astype(F32)
        for d in far_first:
            z_copy(1, d, scan_out, scan_in, ctx).start()
        scan_in[ctx] = scan_out[ctx]
        z_all(1, scan_out, scan_in).wait_recv()

    grow = jnp.exp(b_col)
    for h in range(HEAD_DEV):
        at = slice(h * HEAD_DIM, (h + 1) * HEAD_DIM)
        whole = inner[:, at]
        if n_ctx > 1:
            pieces = [scan_in[h * per_head + p] for p in range(per_head)]
            incoming = jnp.concatenate(pieces, axis=0) if per_head > 1 else pieces[0]
            carried = jnp.dot(q_ref[:, at], incoming, preferred_element_type=F32)
            whole = whole + grow[:, h : h + 1] * carried
        split = whole.astype(BF16).reshape(n_y, 2, tok, HEAD_DIM)
        for c in range(2):
            attended[c, :, at] = split[:, c].reshape(n_y * tok, HEAD_DIM)
    pair_a = remote(
        attended.at[1 - core], att_in, pair_send.at[1], pair_recv.at[chunks], exp=exp_at(0, 1)
    )
    pair_a.start()
    loads[5].wait()
    loads[6].wait()

    right, left = exp_at(1), exp_at(-1)
    span = cols // 2

    def ring_copy(way, step, i):
        return remote(
            ring_out.at[way, step, i],
            ring_in.at[way, step, i],
            ring_send.at[2],
            ring_recv.at[way, step, i],
            exp=left if way else right,
        )

    def half_copy(way, step, i, p):
        part = pl.ds(p * span, span)
        return remote(
            ring_out.at[way, step, i, :, part],
            ring_in.at[way, step, i, :, part],
            ring_send.at[step],
            ring_recv.at[way, step, i],
            exp=left if way else right,
        )

    def arrived(way, step, i):
        if step > 0:
            ring_copy(way, step, i).wait_recv()
        else:
            half_copy(way, 0, i, way).wait_recv()

    def dest(way, step):
        away = half - step
        return (y - away + n_y) % n_y if way else (y + away) % n_y

    def first_send(way, step, i, p):
        part = slice(p * span, (p + 1) * span)
        ring_out[way, step, i, :, part] = prod[i, dest(way, step), :, part].astype(BF16)
        half_copy(way, step, i, p).start()

    def pass_on(step, i):
        for way in range(2):
            arrived(way, step - 1, i)
            total = prod[i, dest(way, step)] + ring_in[way, step - 1, i].astype(F32)
            ring_out[way, step, i] = total.astype(BF16)
            ring_copy(way, step, i).start()

    lag = 2 if half > 1 else 0

    @pl.loop(0, chunks + lag)
    def _(i):
        @pl.when(i < chunks)
        def _():
            at = columns(i)
            term = jnp.dot(attended[core], weights[0, :, at], preferred_element_type=F32)

            @pl.when(i == 0)
            def _():
                pair_a.wait_recv()

            pair_w(i).wait_recv()
            term = term + jnp.dot(att_in[...], weights[1, :, at], preferred_element_type=F32)
            prod[i] = term.reshape(n_y, tok, cols)
            for way in range(2):
                first_send(way, 0, i, way)
            if half > 1:
                for way in range(2):
                    first_send(way, 1, i, 1 - way)

        if half > 1:

            @pl.when(i >= lag)
            def _():
                now = i - lag
                for way in range(2):
                    part = slice(way * span, (way + 1) * span)
                    half_copy(way, 0, now, way).wait_recv()
                    total = prod[now, dest(way, 1), :, part]
                    total = total + ring_in[way, 0, now, :, part].astype(F32)
                    ring_out[way, 1, now, :, part] = total.astype(BF16)
                    half_copy(way, 1, now, way).start()

    for step in range(2, half):

        @pl.loop(0, chunks)
        def _(i, step=step):
            pass_on(step, i)

    def shift_copy(i):
        return remote(
            shift_out.at[i],
            shift_in.at[i],
            shift_send.at[0],
            shift_recv.at[i],
            section=(sec + 1) % n_sec,
        )

    groups = (pl.ds(0, RAW * cols), pl.ds(RAW * cols, width - RAW * cols))

    def slot_copy(g, dy, flip):
        peer = exp_at(dy, flip)
        return remote(
            placed.at[peer, :, groups[g]],
            rows_out.at[exp, :, groups[g]],
            slot_send.at[g],
            slot_recv.at[g],
            exp=peer,
        )

    def own_copy(g):
        return pltpu.make_async_copy(
            placed.at[exp, :, groups[g]], rows_out.at[exp, :, groups[g]], own_sem.at[g]
        )

    order = sorted(range(1, n_y), key=lambda d: -min(d, n_y - d)) + [0]
    others = [(dy, flip) for dy in order for flip in (0, 1) if (dy, flip) != (0, 0)]

    def place(i):
        slots = jnp.dot(picks[...], shift_in[i], preferred_element_type=F32)
        placed[:, :, columns(i)] = slots.reshape(n_exp, 8, cols)[:, 0:CAP].astype(BF16)

    def send_slots(g):
        for dy, flip in others:
            slot_copy(g, dy, flip).start()
        own_copy(g).start()

    squares[...] = jnp.zeros_like(squares)

    def add_squares(i):
        if n_sec > 1:
            shift_copy(i).wait_recv()
        wide = shift_in[i].astype(F32)
        squares[...] += jnp.sum(wide * wide, axis=-1, keepdims=True)

    @pl.loop(0, chunks)
    def _(i):
        arrived(0, half - 1, i)
        arrived(1, half - 1, i)
        at = columns(i)
        for p in range(2):
            part = slice(p * span, (p + 1) * span)
            total = prod[i, y, :, part]
            for way in range(2):
                if half > 1 or way == p:
                    total = total + ring_in[way, half - 1, i, :, part].astype(F32)
            wide = res_ref[:, pl.ds(pl.multiple_of(i * cols + p * span, 128), span)]
            shift_out[i, :, part] = (total + wide.astype(F32)).astype(BF16)
        if n_sec > 1:
            shift_copy(i).start()
        else:
            shift_in[i] = shift_out[i]

        @pl.when(jnp.logical_and(i >= 2, i < RAW + 2))
        def _():
            now = i - 2
            add_squares(now)
            place(now)

            @pl.when(now == RAW - 1)
            def _():
                send_slots(0)

    @pl.loop(RAW, chunks)
    def _(i):
        add_squares(i)

    loads[7].wait()
    loads[8].wait()
    factor = lax.rsqrt(squares[:, 0:1] / width + EPS)
    logits = jnp.zeros((n_exp, tok), F32)
    for i in range(chunks):
        at = slice(i * cols, (i + 1) * cols)
        normed = (shift_in[i].astype(F32) * factor * gain_ref[:, at]).astype(BF16)
        if i >= RAW:
            shift_in[i] = normed
        logits = logits + contract(router_ref[:, at], normed, ((1,), (1,)))
    picked0 = jnp.sum(logits * is_first, axis=0, keepdims=True)
    picked1 = jnp.sum(logits * (match - is_first), axis=0, keepdims=True)
    gate0 = 1.0 / (1.0 + jnp.exp(picked1 - picked0))
    gate1 = 1.0 - gate0
    diagonal = (iota((tok, tok), 0) == iota((tok, tok), 1)).astype(F32)
    lying = jnp.sum(diagonal * factor, axis=0, keepdims=True)
    first8 = jnp.dot(spread, is_first.astype(BF16), preferred_element_type=F32)
    info = jnp.where(line < CAP, lying, jnp.where(first8 > 0.5, gate0, gate1))
    info = jnp.where(codes == (line % CAP).astype(F32), info, 0.0)
    info = jnp.sum(info, axis=-1, keepdims=True)
    meta_out[...] = jnp.broadcast_to(info, (slot_rows, 128)).reshape(n_exp, 8, 128)

    for dy, flip in others:
        peer = exp_at(dy, flip)
        remote(
            meta_out.at[peer], meta_in.at[exp], meta_send.at[0], meta_recv.at[0], exp=peer
        ).start()
    own_meta = pltpu.make_async_copy(meta_out.at[exp], meta_in.at[exp], own_sem.at[2])
    own_meta.start()

    @pl.loop(RAW, chunks)
    def _(i):
        place(i)

    send_slots(1)

    pair_a.wait_send()
    remote(
        w_hbm, weights.at[1], pair_send.at[0], pair_recv.at[0], exp=exp_at(0, 1)
    ).wait_send()
    if n_ctx > 1:
        z_all(0, state_out, state_in).wait_send()
        z_all(1, scan_out, scan_in).wait_send()

    for step in range(min(half, 2)):
        sent = ring_out.at[0, 0] if step == 0 else ring_out.at[:, 1]
        into = ring_in.at[0, 0] if step == 0 else ring_in.at[:, 1]
        remote(sent, into, ring_send.at[step], ring_recv.at[0, 0, 0], exp=right).wait_send()
    if half > 2:
        later = pl.ds(2, half - 2)
        remote(
            ring_out.at[:, later],
            ring_in.at[:, later],
            ring_send.at[2],
            ring_recv.at[0, 0, 0],
            exp=right,
        ).wait_send()
    if n_sec > 1:
        remote(
            shift_out, shift_in, shift_send.at[0], shift_recv.at[0], section=(sec + 1) % n_sec
        ).wait_send()
    own_meta.wait()
    meta_all = remote(
        meta_out.at[pl.ds(0, n_exp - 1)],
        meta_in.at[pl.ds(0, n_exp - 1)],
        meta_send.at[0],
        meta_recv.at[0],
        exp=right,
    )
    meta_all.wait_send()
    meta_all.wait_recv()
    for g in range(2):
        own_copy(g).wait()
        most = pl.ds(0, n_exp - 1)
        slots_all = remote(
            placed.at[most, :, groups[g]],
            rows_out.at[most, :, groups[g]],
            slot_send.at[g],
            slot_recv.at[g],
            exp=right,
        )
        slots_all.wait_send()
        slots_all.wait_recv()


def finish(rows_in, meta, gain, rows_out, gates_out, scaled, sem):
    n_exp, _, width = rows_in.shape
    head = RAW * COLS
    rest = pltpu.make_async_copy(
        rows_in.at[:, :, head:width], rows_out.at[:, :, head:width], sem.at[0]
    )
    rest.start()
    wide = rows_in[:, :, 0:head].astype(F32) * meta[:, 0:CAP, 0:1]
    scaled[...] = (wide * gain[:, 0:head].reshape(1, 1, head)).astype(BF16)
    first = pltpu.make_async_copy(scaled, rows_out.at[:, :, 0:head], sem.at[1])
    first.start()
    lane = iota((CAP, n_exp), 1)
    gates = jnp.zeros((CAP, n_exp), F32)
    for j in range(n_exp):
        gates = jnp.where(lane == j, meta[j, CAP : 2 * CAP, 0:n_exp], gates)
    gates_out[...] = gates.astype(BF16)
    rest.wait()
    first.wait()


def on_device(
    sizes, queries, keys_in, values, decay_rate, out_weight, residual, norm_gain, router, expert_ids
):
    n_sec, n_ctx, n_exp = sizes
    length, inner_width = queries.shape[1:]
    width = out_weight.shape[-1]
    tok = residual.shape[1]
    n_y = n_exp // 2
    half = n_y // 2
    cols = COLS
    chunks = width // cols
    rows = HEAD_DEV * HEAD_DIM // n_ctx
    any_space = pl.BlockSpec(memory_space=pl.ANY)
    dma = pltpu.SemaphoreType.DMA
    vmem_space = pl.BlockSpec(memory_space=pltpu.VMEM)
    slots, meta = pl.pallas_call(
        functools.partial(kernel, (n_sec, n_ctx, n_exp, length, width, cols)),
        out_shape=(
            jax.ShapeDtypeStruct((n_exp, CAP, width), BF16),
            jax.ShapeDtypeStruct((n_exp, 8, 128), F32),
        ),
        in_specs=[pl.BlockSpec(memory_space=pltpu.HBM)] * 9,
        out_specs=(any_space, any_space),
        scratch_shapes=[
            pltpu.VMEM((length, inner_width), BF16),
            pltpu.VMEM((length, inner_width), BF16),
            pltpu.VMEM((length, inner_width), BF16),
            pltpu.VMEM((HEAD_DEV, length), F32),
            pltpu.VMEM((tok, width), BF16),
            pltpu.VMEM((1, width), F32),
            pltpu.VMEM((n_exp, width), BF16),
            pltpu.VMEM((2, tok), jnp.int32),
            pltpu.VMEM((2, inner_width, width), BF16),
            pltpu.VMEM((length, inner_width), F32),
            pltpu.VMEM((2, n_y * tok, inner_width), BF16),
            pltpu.VMEM((n_y * tok, inner_width), BF16),
            pltpu.VMEM((chunks, n_y, tok, cols), F32),
            pltpu.VMEM((n_ctx, rows + 16, HEAD_DIM), BF16),
            pltpu.VMEM((n_ctx, rows + 16, HEAD_DIM), BF16),
            pltpu.VMEM((n_ctx, rows, HEAD_DIM), BF16),
            pltpu.VMEM((n_ctx, rows, HEAD_DIM), BF16),
            pltpu.VMEM((2, half, chunks, tok, cols), BF16),
            pltpu.VMEM((2, half, chunks, tok, cols), BF16),
            pltpu.VMEM((chunks, tok, cols), BF16),
            pltpu.VMEM((chunks, tok, cols), BF16),
            pltpu.VMEM((n_exp, CAP, width), BF16),
            pltpu.VMEM((n_exp * 8, tok), BF16),
            pltpu.VMEM((tok, 128), F32),
            pltpu.VMEM((n_exp, 8, 128), F32),
            dma((9,)),
            dma((2,)),
            dma((chunks + 1,)),
            dma((2,)),
            dma((2,)),
            dma((3,)),
            dma((2, half, chunks)),
            dma((1,)),
            dma((chunks,)),
            dma((2,)),
            dma((2,)),
            dma((1,)),
            dma((1,)),
            dma((3,)),
        ],
        compiler_params=pltpu.CompilerParams(
            collective_id=0, has_side_effects=True, vmem_limit_bytes=VMEM_MIB * 2**20
        ),
    )(
        *(
            pltpu.with_memory_space_constraint(x, pltpu.HBM)
            for x in (
                queries[0],
                keys_in[0],
                values[0],
                decay_rate[0],
                out_weight[0],
                residual[0],
                norm_gain,
                router[0].T,
                expert_ids[0].T,
            )
        )
    )
    rows_out, gates = pl.pallas_call(
        finish,
        out_shape=(
            jax.ShapeDtypeStruct((n_exp, CAP, width), BF16),
            jax.ShapeDtypeStruct((CAP, n_exp), BF16),
        ),
        in_specs=[vmem_space] * 3,
        out_specs=(any_space, vmem_space),
        scratch_shapes=[pltpu.VMEM((n_exp, CAP, RAW * cols), BF16), dma((2,))],
        compiler_params=pltpu.CompilerParams(vmem_limit_bytes=8 * 2**20),
    )(slots, meta, norm_gain)
    return (rows_out[None, None, None], gates.T[None, None, None])


def solution(mesh):
    sizes = tuple(mesh.shape[a] for a in ("section", "ctx", "exp"))
    placed = (
        P("section", "ctx", "exp"),
        P("section", "ctx", "exp"),
        P("section", "ctx", "exp"),
        P("section", "exp", "ctx"),
        P("section", "exp", None),
        P("section", ("ctx", "exp"), None),
        P("section", None),
        P("section", None, None),
        P("section", ("ctx", "exp"), None),
    )
    return jax.shard_map(
        functools.partial(on_device, sizes),
        mesh=mesh,
        in_specs=placed,
        out_specs=(
            P("section", "ctx", "exp", None, None, None),
            P("section", "ctx", "exp", None, None),
        ),
        check_vma=False,
    )
```
